32 devices in a mesh: grp: 2 (over x), had: 16 (over z, y, core).
Axes of the slice: x: 2, y: 2, z: 4, core: 2. Of those that a mesh axis runs over, the one named last changes fastest.
Arguments:
- source_slabs: bfloat16 [512, 128, 128], P(('grp', 'had')), parts along dimension 0, may hold values from -6 to 6
- sink_slabs: bfloat16 [512, 128, 128], P(('grp', 'had')), parts along dimension 0, may hold values from -6 to 6
- perambulators: bfloat16 [4, 2, 128, 128], P('grp'), parts along dimension 0, may hold values from -0.5 to 0.5
- send_pick: int32 [32, 16], P(('grp', 'had')), parts along dimension 0, may hold values from 0 to 15
- graph_slot: int32 [32, 512, 2], P(('grp', 'had')), parts along dimension 0, may hold values from 0 to 15
- graph_sink: int32 [32, 512, 2], P(('grp', 'had')), parts along dimension 0, may hold values from 0 to 15
- graph_count: int32 [32], P(('grp', 'had')), parts along dimension 0, may hold values from 64 to 512, as said below
- pair_list: int32 [256, 2], P(('grp', 'had')), parts along dimension 0, may hold values from 0 to 15
Outputs:
- edge_matrices: bfloat16 [32, 128, 128], P(('grp', 'had')), parts along dimension 0
- pair_products: bfloat16 [256, 128, 128], P(('grp', 'had')), parts along dimension 0
The draws below stay inside these ranges and needn't reach their ends.
There are 2 independent parts, one for each index of `grp`. The reference program is written for one: setup_inputs(seed, part) draws one part's arguments, and reference() takes and returns one part's arrays. A program takes and returns all parts, laid end to end along the dimension named above; each array names one. Nothing has to cross between parts.
Inputs may be any that keep to these rules, and one draw needn't show every extreme that they name: Some reader uses all 512 graph slots; slots from graph_count on are unused.
All inputs are finite; a program needn't handle non-finite values.
Results may differ from the reference program's by a relative error of at most 0.012.
Values may be sent and summed in bfloat16 or wider, within the bound.
A program may use at most 64 MiB of HBM per device.

```python
import math
import jax
import jax.numpy as jnp
from jax import lax

EVECS = 128
SLAB_DEV = 16
GRAPH_DEV = 512
READERS = 16
SLABS = 256
TSLICES = 2
PAIRS = 128


def draw_graph_count(key, part):
    shift_key, top_key = jax.random.split(jax.random.fold_in(key, 17))
    levels = jnp.array([GRAPH_DEV, GRAPH_DEV // 2, GRAPH_DEV // 4, GRAPH_DEV // 8], dtype=jnp.int32)
    chosen = levels[jax.random.randint(shift_key, (READERS,), 0, 4)]
    busiest = jax.random.randint(top_key, (), 0, READERS)
    return jnp.where(jnp.arange(READERS) == busiest, GRAPH_DEV, chosen).astype(jnp.int32)


def with_ends(drawn, own_key, smallest, top_value):
    dims = drawn.shape
    place = [jax.random.randint(jax.random.fold_in(own_key, axis), (), 0, dims[axis]) for axis in range(len(dims))]
    drawn = drawn.at[tuple(place)].set(smallest)
    longest = dims.index(max(dims))
    place[longest] = (place[longest] + 1) % dims[longest]
    return drawn.at[tuple(place)].set(top_value)


def block_scale(key, shape, cuts, least, top_value):
    gain = 1.0
    for position, shards_of in cuts:
        heights = jax.random.uniform(jax.random.fold_in(jax.random.fold_in(key, 6), position), (shards_of,), jnp.float32, least / len(cuts), top_value / len(cuts))
        gain = gain * jnp.repeat(jnp.exp(heights), shape[position] // shards_of).reshape((-1,) + (1,) * (len(shape) - 1 - position))
    return gain


def centred(own_key, dims, width, limit, shards=(), kind=jnp.bfloat16):
    level = block_scale(own_key, dims, shards, -0.22, 0.18) if shards else 1.0
    values = jax.random.normal(own_key, dims, jnp.float32) * width * level
    return jnp.minimum(jnp.maximum(values, -limit), limit).astype(kind)


def setup_inputs(seed: int = 0, part: int = 0) -> dict:
    key_of = jax.random.split(jax.random.key(seed), 9)
    part_splits = jax.random.split(jax.random.fold_in(key_of[8], part), 9)
    source_slabs = centred(part_splits[0], (SLABS, EVECS, EVECS), 1.0, 6.0, ((0, 16),))
    sink_slabs = centred(part_splits[1], (SLABS, EVECS, EVECS), 1.0, 6.0, ((0, 16),))
    perambulators = centred(part_splits[2], (TSLICES, 2, EVECS, EVECS), EVECS ** -0.5, 0.5)
    send_pick = with_ends(jax.random.randint(part_splits[3], (READERS, READERS), 0, SLAB_DEV), jax.random.fold_in(part_splits[3], 1), 0, SLAB_DEV - 1).astype(jnp.int32)
    graph_slot = with_ends(jax.random.randint(part_splits[4], (READERS, GRAPH_DEV, 2), 0, READERS), jax.random.fold_in(part_splits[4], 1), 0, READERS - 1).astype(jnp.int32)
    graph_sink = with_ends(jax.random.randint(part_splits[5], (READERS, GRAPH_DEV, 2), 0, SLAB_DEV), jax.random.fold_in(part_splits[5], 1), 0, SLAB_DEV - 1).astype(jnp.int32)
    graph_count = draw_graph_count(jax.random.fold_in(jax.random.fold_in(key_of[8], part), 71), part)
    pair_list = with_ends(jax.random.randint(part_splits[7], (PAIRS, 2), 0, READERS), jax.random.fold_in(part_splits[7], 1), 0, READERS - 1).astype(jnp.int32)
    return dict(source_slabs=source_slabs, sink_slabs=sink_slabs, perambulators=perambulators, send_pick=send_pick, graph_slot=graph_slot, graph_sink=graph_sink, graph_count=graph_count, pair_list=pair_list)


def rotated_slabs(source_slabs, perambulators):
    grouped = source_slabs.reshape(TSLICES, EVECS, EVECS, EVECS).astype(jnp.float32)
    first_turn = jnp.einsum('txa,tcab->tcxb', perambulators[:, 0].astype(jnp.float32), grouped).astype(jnp.bfloat16)
    second_turn = jnp.einsum('tcxb,tyb->tcxy', first_turn.astype(jnp.float32), perambulators[:, 1].astype(jnp.float32))
    return second_turn.astype(jnp.bfloat16).reshape(SLABS, EVECS, EVECS)

def reference(source_slabs, sink_slabs, perambulators, send_pick, graph_slot, graph_sink, graph_count, pair_list):
    rotated = rotated_slabs(source_slabs, perambulators)
    root_scale = 1.0 / math.sqrt(EVECS)
    edge_scale = 1.0 / math.sqrt(EVECS * GRAPH_DEV)
    owners = jnp.arange(READERS, dtype=jnp.int32)

    def reader_edge(packed):
        reader, slot_rows, sink_rows, graph_total = packed
        pick_column = lax.dynamic_index_in_dim(send_pick, reader, 1, keepdims=False)
        received = rotated[(owners * SLAB_DEV + pick_column).astype(jnp.int32)]
        resident = lax.dynamic_slice_in_dim(sink_slabs, (reader * SLAB_DEV).astype(jnp.int32), SLAB_DEV, 0)

        def factor(slots, sinks):
            product = jnp.einsum('gxb,gab->gxa', resident[sinks].astype(jnp.float32), received[slots].astype(jnp.float32))
            return (product * root_scale).astype(jnp.bfloat16)
        is_valid = (jnp.arange(GRAPH_DEV, dtype=jnp.int32) < graph_total).astype(jnp.float32)
        left_side = factor(slot_rows[:, 0], sink_rows[:, 0]).astype(jnp.float32) * is_valid[:, None, None]
        right_side = factor(slot_rows[:, 1], sink_rows[:, 1]).astype(jnp.float32)
        summed = jnp.einsum('gxa,gay->xy', left_side, right_side)
        return (summed * edge_scale).astype(jnp.bfloat16)
    edge_matrices = lax.map(reader_edge, (owners, graph_slot, graph_sink, graph_count))
    left_edges = edge_matrices[pair_list[:, 0]].astype(jnp.float32)
    right_edges = edge_matrices[pair_list[:, 1]].astype(jnp.float32)
    pair_products = (jnp.einsum('pxa,pay->pxy', left_edges, right_edges) * root_scale).astype(jnp.bfloat16)
    return (edge_matrices, pair_products)
```

```python
import functools
import math

import jax
import jax.numpy as jnp
from jax import lax
from jax.experimental import pallas as pl
from jax.experimental.pallas import tpu as pltpu
from jax.sharding import PartitionSpec as P


def looped_shards(
    source_slabs,
    sink_slabs,
    perambulators,
    send_pick,
    graph_slot,
    graph_sink,
    graph_count,
    pair_list,
):
    my_index = lax.axis_index("had")
    evecs = source_slabs.shape[1]
    per_device = source_slabs.shape[0]
    root_scale = 1.0 / math.sqrt(evecs)
    edge_scale = 1.0 / math.sqrt(evecs * graph_slot.shape[1])
    timeslice = my_index * per_device // evecs
    local_peram = lax.dynamic_index_in_dim(perambulators, timeslice, 0, keepdims=False)
    first_turn = jnp.einsum(
        "xa,jab->xjb", local_peram[0], source_slabs, preferred_element_type=jnp.float32
    ).astype(jnp.bfloat16)
    pick_row = send_pick[0]
    second_turn = jnp.einsum(
        "xjb,yb->xjy", first_turn, local_peram[1], preferred_element_type=jnp.float32
    ).astype(jnp.bfloat16)
    outgoing = jnp.take(second_turn, pick_row, axis=1)
    received = lax.all_to_all(outgoing, "had", split_axis=1, concat_axis=1, tiled=True)
    graph_rows = graph_slot.shape[1]
    block_width = min(64, graph_rows)
    slot_table = graph_slot[0]
    sink_table = graph_sink[0]
    graph_total = graph_count[0]

    def factor(slots, sinks):
        gathered = jnp.take(received, slots, axis=1)
        resident = jnp.take(sink_slabs, sinks, axis=0)
        product = jnp.einsum("gxb,agb->gxa", resident, gathered, preferred_element_type=jnp.float32)
        return (product * root_scale).astype(jnp.bfloat16)

    def accumulate(block_index, running_sum):
        offset = block_index * block_width
        slots = lax.dynamic_slice_in_dim(slot_table, offset, block_width, 0)
        sinks = lax.dynamic_slice_in_dim(sink_table, offset, block_width, 0)
        is_valid = (offset + jnp.arange(block_width, dtype=jnp.int32) < graph_total).astype(
            jnp.bfloat16
        )
        left_side = factor(slots[:, 0], sinks[:, 0]) * is_valid[:, None, None]
        right_side = factor(slots[:, 1], sinks[:, 1])
        return running_sum + jnp.einsum(
            "gxa,gay->xy", left_side, right_side, preferred_element_type=jnp.float32
        )

    block_count = (graph_total + block_width - 1) // block_width
    summed = lax.fori_loop(0, block_count, accumulate, jnp.zeros((evecs, evecs), jnp.float32))
    edge_local = (summed * edge_scale).astype(jnp.bfloat16)[None]
    left_ids = pair_list[:, 0]
    right_ids = pair_list[:, 1]
    shard_rows = lax.all_gather(edge_local, "had", axis=0, tiled=True)
    row_ids = jnp.arange(shard_rows.shape[0], dtype=jnp.int32)
    left_select = (left_ids[:, None] == row_ids[None, :]).astype(jnp.bfloat16)
    right_select = (right_ids[:, None] == row_ids[None, :]).astype(jnp.bfloat16)
    left_part = jnp.einsum(
        "pn,nxy->pxy", left_select, shard_rows, preferred_element_type=jnp.float32
    )
    right_part = jnp.einsum(
        "pn,nxy->pxy", right_select, shard_rows, preferred_element_type=jnp.float32
    )
    left_edges = left_part.astype(jnp.bfloat16)
    right_edges = right_part.astype(jnp.bfloat16)
    product = jnp.einsum(
        "pxa,pay->pxy", left_edges, right_edges, preferred_element_type=jnp.float32
    )
    pair_products = (product * root_scale).astype(jnp.bfloat16)
    return (edge_local, pair_products)


NT = (((1,), (1,)), ((), ()))
UNROLL = 256


def flip(index, step):
    flipped = index
    bit = 1
    while bit <= step:
        if step & bit:
            flipped = flipped + bit * (1 - 2 * (index // bit % 2))
        bit *= 2
    return flipped


def fused_kernel(
    n,
    graphs,
    pick_in,
    slot_in,
    graph_sink_in,
    count_in,
    pair_in,
    peram_in,
    source_in,
    sink_in,
    edge_out,
    product_out,
    edges,
    outgoing,
    received,
    table,
    slot_ref,
    graph_sink_ref,
    index_ref,
    pick_ref,
    count_ref,
    pair_ref,
    graph_ref,
    peram_ref,
    source_ref,
    sink_ref,
    load_sem,
    send_sem,
    recv_sem,
    edge_recv_sem,
):
    me = lax.axis_index("had")
    per_device, evecs, _ = source_ref.shape
    root_scale = 1.0 / math.sqrt(evecs)
    edge_scale = 1.0 / math.sqrt(evecs * graphs)
    sinks = sink_ref.shape[0]

    def at(peer):
        return dict(device_id={"had": peer}, device_id_type=pl.DeviceIdType.MESH)

    barrier = pltpu.get_barrier_semaphore()
    for step in range(n - 1, 0, -1):
        pl.semaphore_signal(barrier, inc=1, **at(flip(me, step)))

    loads = {}
    for name, source, target in (
        ("pick", pick_in, pick_ref),
        ("peram", peram_in, peram_ref),
        ("source", source_in, source_ref),
        ("slot", slot_in, slot_ref),
        ("graph_sink", graph_sink_in, graph_sink_ref),
        ("count", count_in, count_ref),
        ("sink", sink_in, sink_ref),
        ("pair", pair_in, pair_ref),
    ):
        loads[name] = pltpu.make_async_copy(source, target, load_sem.at[len(loads)])
        loads[name].start()
    with jax.named_scope("load"):
        for name in ("pick", "peram", "source"):
            loads[name].wait()

    timeslice = me * per_device // evecs
    first = peram_ref[timeslice, 0]
    second = peram_ref[timeslice, 1]
    copies = {}

    def rotate(steps):
        halves = []
        for step in steps:
            slab = source_ref[pick_ref[0, flip(me, step)]]
            half = jnp.dot(first, slab, preferred_element_type=jnp.float32)
            halves.append(half.astype(jnp.bfloat16))
        for step, half in zip(steps, halves):
            turned = lax.dot_general(half, second, NT, preferred_element_type=jnp.float32)
            target = outgoing if step else received
            target[flip(me, step)] = turned.astype(jnp.bfloat16)

    def send(steps):
        for step in steps:
            if step == 0:
                continue
            peer = flip(me, step)
            copies[step] = pltpu.make_async_remote_copy(
                src_ref=outgoing.at[peer],
                dst_ref=received.at[me],
                send_sem=send_sem.at[0],
                recv_sem=recv_sem.at[step // 2],
                **at(peer),
            )
            copies[step].start()

    def both_cores(buffer, peer_chip, semaphore):
        pair = buffer.at[pl.ds(flip(me, 2 * peer_chip) // 2 * 2, 2)]
        if peer_chip == 0:
            pair = buffer.at[flip(me, 1)]
        return pltpu.make_async_remote_copy(
            src_ref=pair,
            dst_ref=pair,
            send_sem=send_sem.at[0],
            recv_sem=semaphore.at[peer_chip],
            **at(flip(me, 1)),
        )

    def all_sent(semaphore):
        pltpu.make_async_remote_copy(
            src_ref=outgoing.at[pl.ds(1, n - 1)],
            dst_ref=received.at[pl.ds(1, n - 1)],
            send_sem=semaphore,
            recv_sem=recv_sem.at[0],
            **at(flip(me, 1)),
        ).wait_send()

    order = [*range(n // 2, n), *range(n // 4, n // 2), *range(n // 4)]
    group = 4
    for at_group in range(0, n, group):
        steps = order[at_group : at_group + group]
        with jax.named_scope(f"rotate{at_group}"):
            rotate(steps)
        if at_group == 0:
            with jax.named_scope("meet"):
                pl.semaphore_wait(barrier, n - 1)
        send(steps)

    with jax.named_scope("index"):
        for name in ("slot", "graph_sink", "count"):
            loads[name].wait()
        graph_ids = lax.broadcasted_iota(jnp.int32, slot_ref.shape, 1)
        index_ref[...] = jnp.where(
            graph_ids < count_ref[0], slot_ref[...] * sinks + graph_sink_ref[...], n * sinks
        )
        index_load = pltpu.make_async_copy(index_ref, graph_ref, load_sem.at[len(loads)])
        index_load.start()
        table[n * sinks] = jnp.zeros((evecs, evecs), jnp.bfloat16)
        rows = 4
        loads["sink"].wait()
        loads["pair"].wait()
        index_load.wait()

    for chip in range(n // 2):
        with jax.named_scope(f"arrive{chip}"):
            both_cores(received, chip, recv_sem).wait_recv()
        base = (flip(me, 2 * chip)) // 2 * 2
        both = received[pl.ds(base, 2)].reshape(2 * evecs, evecs)
        for block in range(sinks // rows):
            left = sink_ref[block * rows : (block + 1) * rows].reshape(rows * evecs, evecs)
            product = lax.dot_general(left, both, NT, preferred_element_type=jnp.float32)
            scaled = (product * root_scale).astype(jnp.bfloat16)
            for core in range(2):
                part = scaled[:, core * evecs : (core + 1) * evecs].reshape(rows, evecs, evecs)
                table[pl.ds((base + core) * sinks + block * rows, rows)] = part
    all_sent(send_sem.at[0])

    def graph_step(block, total):
        start = UNROLL * block
        left = [table[graph_ref[0, start + graph]] for graph in range(UNROLL)]
        right = [table[graph_ref[1, start + graph]] for graph in range(UNROLL)]
        return total + jnp.dot(
            jnp.concatenate(left, axis=1),
            jnp.concatenate(right, axis=0),
            preferred_element_type=jnp.float32,
        )

    with jax.named_scope("graphs"):
        total = lax.fori_loop(
            0, graphs // UNROLL, graph_step, jnp.zeros((evecs, evecs), jnp.float32)
        )
    edge = (total * edge_scale).astype(jnp.bfloat16)
    edges[me] = edge


    def pass_on(step, peer_step, semaphore):
        owner = flip(me, step)
        pltpu.make_async_remote_copy(
            src_ref=edges.at[owner],
            dst_ref=edges.at[owner],
            send_sem=send_sem.at[1],
            recv_sem=semaphore,
            **at(flip(me, peer_step)),
        ).start()

    def arrived(step):
        pltpu.make_async_remote_copy(
            src_ref=edges.at[me],
            dst_ref=edges.at[flip(me, step)],
            send_sem=send_sem.at[1],
            recv_sem=edge_recv_sem.at[step // 2],
            **at(flip(me, 1)),
        ).wait_recv()

    for step in range(n - 2, 0, -2):
        pass_on(0, step, edge_recv_sem.at[step // 2])
    pass_on(0, 1, edge_recv_sem.at[0])
    edge_out[0] = edge
    for step in range(2, n, 2):
        with jax.named_scope(f"gather{step}"):
            arrived(step)
        pass_on(step, 1, edge_recv_sem.at[0])
    with jax.named_scope("partner"):
        pltpu.make_async_remote_copy(
            src_ref=edges.at[pl.ds(0, n // 2)],
            dst_ref=edges.at[pl.ds(0, n // 2)],
            send_sem=send_sem.at[1],
            recv_sem=edge_recv_sem.at[0],
            **at(flip(me, 1)),
        ).wait_recv()
    with jax.named_scope("pairs"):
        for pair in range(product_out.shape[0]):
            product = jnp.dot(
                edges[pair_ref[0, pair]],
                edges[pair_ref[1, pair]],
                preferred_element_type=jnp.float32,
            )
            product_out[pair] = (product * root_scale).astype(jnp.bfloat16)
    all_sent(send_sem.at[1])


def store_kernel(edge_in, product_in, edge_out, product_out, store_sem):
    edge_copy = pltpu.make_async_copy(edge_in, edge_out, store_sem.at[0])
    product_copy = pltpu.make_async_copy(product_in, product_out, store_sem.at[1])
    edge_copy.start()
    product_copy.start()
    edge_copy.wait()
    product_copy.wait()


def fused_shards(
    n,
    source_slabs,
    sink_slabs,
    perambulators,
    send_pick,
    graph_slot,
    graph_sink,
    graph_count,
    pair_list,
):
    sinks, evecs, _ = sink_slabs.shape
    graphs = graph_slot.shape[1]
    pairs = pair_list.shape[0]
    vmem = pl.BlockSpec(memory_space=pltpu.VMEM)
    hbm = pl.BlockSpec(memory_space=pltpu.HBM)
    slab = (evecs, evecs)
    held = pl.pallas_call(
        functools.partial(fused_kernel, n, graphs),
        out_shape=(
            pltpu.VMEM((1, *slab), jnp.bfloat16),
            pltpu.VMEM((pairs, *slab), jnp.bfloat16),
        ),
        in_specs=[hbm] * 8,
        out_specs=(vmem, vmem),
        scratch_shapes=[
            pltpu.VMEM((n, *slab), jnp.bfloat16),
            pltpu.VMEM((n, *slab), jnp.bfloat16),
            pltpu.VMEM((n, *slab), jnp.bfloat16),
            pltpu.VMEM((n * sinks + 1, *slab), jnp.bfloat16),
            pltpu.VMEM((2, graphs), jnp.int32),
            pltpu.VMEM((2, graphs), jnp.int32),
            pltpu.VMEM((2, graphs), jnp.int32),
            pltpu.SMEM(send_pick.shape, jnp.int32),
            pltpu.SMEM((1,), jnp.int32),
            pltpu.SMEM((2, pairs), jnp.int32),
            pltpu.SMEM((2, graphs), jnp.int32),
            pltpu.VMEM(perambulators.shape, jnp.bfloat16),
            pltpu.VMEM(source_slabs.shape, jnp.bfloat16),
            pltpu.VMEM(sink_slabs.shape, jnp.bfloat16),
            pltpu.SemaphoreType.DMA((9,)),
            pltpu.SemaphoreType.DMA((2,)),
            pltpu.SemaphoreType.DMA((n // 2,)),
            pltpu.SemaphoreType.DMA((n // 2,)),
        ],
        compiler_params=pltpu.CompilerParams(
            collective_id=0, has_side_effects=True
        ),
        name="contraction",
    )(
        send_pick,
        graph_slot[0].T,
        graph_sink[0].T,
        graph_count,
        pair_list.T,
        perambulators,
        source_slabs,
        sink_slabs,
    )
    return pl.pallas_call(
        store_kernel,
        out_shape=tuple(jax.ShapeDtypeStruct(part.shape, part.dtype) for part in held),
        in_specs=[vmem, vmem],
        out_specs=(hbm, hbm),
        scratch_shapes=[pltpu.SemaphoreType.DMA((2,))],
        compiler_params=pltpu.CompilerParams(vmem_limit_bytes=1024 * 1024),
        name="store",
    )(*(pltpu.with_memory_space_constraint(part, pltpu.VMEM) for part in held))


def shards(readers, source_slabs, sink_slabs, perambulators, *tables):
    slabs = sink_slabs.shape[0]
    graphs = tables[1].shape[1]
    power = readers & (readers - 1) == 0 and readers % 4 == 0
    if power and readers * slabs <= 2 * graphs and graphs % UNROLL == 0 and slabs % 4 == 0:
        return fused_shards(readers, source_slabs, sink_slabs, perambulators, *tables)
    return looped_shards(source_slabs, sink_slabs, perambulators, *tables)


def solution(mesh):
    return jax.shard_map(
        functools.partial(shards, mesh.shape["had"]),
        mesh=mesh,
        in_specs=(
            P(("grp", "had"), None, None),
            P(("grp", "had"), None, None),
            P("grp", None, None, None),
            P(("grp", "had"), None),
            P(("grp", "had"), None, None),
            P(("grp", "had"), None, None),
            P(("grp", "had")),
            P(("grp", "had"), None),
        ),
        out_specs=(P(("grp", "had"), None, None), P(("grp", "had"), None, None)),
        check_vma=False,
    )
```

```python
import functools
import math

import jax
import jax.numpy as jnp
from jax import lax
from jax.experimental import pallas as pl
from jax.experimental.pallas import tpu as pltpu
from jax.sharding import PartitionSpec as P


def looped_shards(
    source_slabs,
    sink_slabs,
    perambulators,
    send_pick,
    graph_slot,
    graph_sink,
    graph_count,
    pair_list,
):
    my_index = lax.axis_index("had")
    evecs = source_slabs.shape[1]
    per_device = source_slabs.shape[0]
    root_scale = 1.0 / math.sqrt(evecs)
    edge_scale = 1.0 / math.sqrt(evecs * graph_slot.shape[1])
    timeslice = my_index * per_device // evecs
    local_peram = lax.dynamic_index_in_dim(perambulators, timeslice, 0, keepdims=False)
    first_turn = jnp.einsum(
        "xa,jab->xjb", local_peram[0], source_slabs, preferred_element_type=jnp.float32
    ).astype(jnp.bfloat16)
    pick_row = send_pick[0]
    second_turn = jnp.einsum(
        "xjb,yb->xjy", first_turn, local_peram[1], preferred_element_type=jnp.float32
    ).astype(jnp.bfloat16)
    outgoing = jnp.take(second_turn, pick_row, axis=1)
    received = lax.all_to_all(outgoing, "had", split_axis=1, concat_axis=1, tiled=True)
    graph_rows = graph_slot.shape[1]
    block_width = min(64, graph_rows)
    slot_table = graph_slot[0]
    sink_table = graph_sink[0]
    graph_total = graph_count[0]

    def factor(slots, sinks):
        gathered = jnp.take(received, slots, axis=1)
        resident = jnp.take(sink_slabs, sinks, axis=0)
        product = jnp.einsum("gxb,agb->gxa", resident, gathered, preferred_element_type=jnp.float32)
        return (product * root_scale).astype(jnp.bfloat16)

    def accumulate(block_index, running_sum):
        offset = block_index * block_width
        slots = lax.dynamic_slice_in_dim(slot_table, offset, block_width, 0)
        sinks = lax.dynamic_slice_in_dim(sink_table, offset, block_width, 0)
        is_valid = (offset + jnp.arange(block_width, dtype=jnp.int32) < graph_total).astype(
            jnp.bfloat16
        )
        left_side = factor(slots[:, 0], sinks[:, 0]) * is_valid[:, None, None]
        right_side = factor(slots[:, 1], sinks[:, 1])
        return running_sum + jnp.einsum(
            "gxa,gay->xy", left_side, right_side, preferred_element_type=jnp.float32
        )

    block_count = (graph_total + block_width - 1) // block_width
    summed = lax.fori_loop(0, block_count, accumulate, jnp.zeros((evecs, evecs), jnp.float32))
    edge_local = (summed * edge_scale).astype(jnp.bfloat16)[None]
    left_ids = pair_list[:, 0]
    right_ids = pair_list[:, 1]
    shard_rows = lax.all_gather(edge_local, "had", axis=0, tiled=True)
    row_ids = jnp.arange(shard_rows.shape[0], dtype=jnp.int32)
    left_select = (left_ids[:, None] == row_ids[None, :]).astype(jnp.bfloat16)
    right_select = (right_ids[:, None] == row_ids[None, :]).astype(jnp.bfloat16)
    left_part = jnp.einsum(
        "pn,nxy->pxy", left_select, shard_rows, preferred_element_type=jnp.float32
    )
    right_part = jnp.einsum(
        "pn,nxy->pxy", right_select, shard_rows, preferred_element_type=jnp.float32
    )
    left_edges = left_part.astype(jnp.bfloat16)
    right_edges = right_part.astype(jnp.bfloat16)
    product = jnp.einsum(
        "pxa,pay->pxy", left_edges, right_edges, preferred_element_type=jnp.float32
    )
    pair_products = (product * root_scale).astype(jnp.bfloat16)
    return (edge_local, pair_products)


NT = (((1,), (1,)), ((), ()))
UNROLL = 256
HALF = 64
HOP = {2: 2, 4: 4, 8: 8, 12: 12, 6: 6, 10: 10, 14: 14, 1: 1, 3: 1, 5: 1, 7: 1, 9: 1, 11: 1, 13: 1, 15: 1}
SENDS = [14,12,10,8,6,4,2,1,3,5,7,9,11,13,15]
WAITS = [2,4,6,8,10,12,14]


def flip(index, step):
    flipped = index
    bit = 1
    while bit <= step:
        if step & bit:
            flipped = flipped + bit * (1 - 2 * (index // bit % 2))
        bit *= 2
    return flipped


def fused_kernel(
    n,
    graphs,
    pick_in,
    slot_in,
    graph_sink_in,
    count_in,
    pair_in,
    peram_in,
    source_in,
    sink_in,
    edge_out,
    product_out,
    edges,
    outgoing,
    received,
    table,
    slot_ref,
    graph_sink_ref,
    index_ref,
    pick_ref,
    count_ref,
    pair_ref,
    graph_ref,
    peram_ref,
    source_ref,
    sink_ref,
    load_sem,
    send_sem,
    recv_sem,
    edge_recv_sem,
):
    me = lax.axis_index("had")
    per_device, evecs, _ = source_ref.shape
    root_scale = 1.0 / math.sqrt(evecs)
    edge_scale = 1.0 / math.sqrt(evecs * graphs)
    sinks = sink_ref.shape[0]

    def at(peer):
        return dict(device_id={"had": peer}, device_id_type=pl.DeviceIdType.MESH)

    barrier = pltpu.get_barrier_semaphore()
    for step in range(n - 1, 0, -1):
        pl.semaphore_signal(barrier, inc=1, **at(flip(me, step)))

    loads = {}
    for name, source, target in (
        ("pick", pick_in, pick_ref),
        ("peram", peram_in, peram_ref),
        ("source", source_in, source_ref),
        ("slot", slot_in, slot_ref),
        ("graph_sink", graph_sink_in, graph_sink_ref),
        ("count", count_in, count_ref),
        ("sink", sink_in, sink_ref),
        ("pair", pair_in, pair_ref),
    ):
        loads[name] = pltpu.make_async_copy(source, target, load_sem.at[len(loads)])
        loads[name].start()
    with jax.named_scope("load"):
        for name in ("pick", "peram", "source"):
            loads[name].wait()

    timeslice = me * per_device // evecs
    first = peram_ref[timeslice, 0]
    second = peram_ref[timeslice, 1]
    copies = {}

    def rotate(steps):
        halves = []
        for step in steps:
            slab = source_ref[pick_ref[0, flip(me, step)]]
            half = jnp.dot(first, slab, preferred_element_type=jnp.float32)
            halves.append(half.astype(jnp.bfloat16))
        for step, half in zip(steps, halves):
            turned = lax.dot_general(half, second, NT, preferred_element_type=jnp.float32)
            target = outgoing if step else received
            target[flip(me, step)] = turned.astype(jnp.bfloat16)

    def send(steps):
        for step in steps:
            if step == 0:
                continue
            peer = flip(me, step)
            copies[step] = pltpu.make_async_remote_copy(
                src_ref=outgoing.at[peer],
                dst_ref=received.at[me],
                send_sem=send_sem.at[0],
                recv_sem=recv_sem.at[step // 2],
                **at(peer),
            )
            copies[step].start()

    def both_cores(buffer, peer_chip, semaphore):
        pair = buffer.at[pl.ds(flip(me, 2 * peer_chip) // 2 * 2, 2)]
        if peer_chip == 0:
            pair = buffer.at[flip(me, 1)]
        return pltpu.make_async_remote_copy(
            src_ref=pair,
            dst_ref=pair,
            send_sem=send_sem.at[0],
            recv_sem=semaphore.at[peer_chip],
            **at(flip(me, 1)),
        )

    def all_sent(semaphore):
        pltpu.make_async_remote_copy(
            src_ref=outgoing.at[pl.ds(1, n - 1)],
            dst_ref=received.at[pl.ds(1, n - 1)],
            send_sem=semaphore,
            recv_sem=recv_sem.at[0],
            **at(flip(me, 1)),
        ).wait_send()

    order = [9, 11, 13, 15, 8, 10, 12, 14, 5, 7, 4, 6, 3, 2, 1, 0]
    group = 4
    for at_group in range(0, n, group):
        steps = order[at_group : at_group + group]
        with jax.named_scope(f"rotate{at_group}"):
            rotate(steps)
        if at_group == 0:
            with jax.named_scope("meet"):
                pl.semaphore_wait(barrier, n - 1)
        send(steps)

    with jax.named_scope("index"):
        for name in ("slot", "graph_sink", "count"):
            loads[name].wait()
        graph_ids = lax.broadcasted_iota(jnp.int32, slot_ref.shape, 1)
        index_ref[...] = jnp.where(
            graph_ids < count_ref[0], slot_ref[...] * sinks + graph_sink_ref[...], n * sinks
        )
        index_load = pltpu.make_async_copy(index_ref, graph_ref, load_sem.at[len(loads)])
        index_load.start()
        table[n * sinks] = jnp.zeros((evecs, evecs), jnp.bfloat16)
        rows = 4
        loads["sink"].wait()
        loads["pair"].wait()
        index_load.wait()

    for chip in range(n // 2):
        with jax.named_scope(f"arrive{chip}"):
            both_cores(received, chip, recv_sem).wait_recv()
        base = (flip(me, 2 * chip)) // 2 * 2
        both = received[pl.ds(base, 2)].reshape(2 * evecs, evecs)
        for block in range(sinks // rows):
            left = sink_ref[block * rows : (block + 1) * rows].reshape(rows * evecs, evecs)
            product = lax.dot_general(left, both, NT, preferred_element_type=jnp.float32)
            scaled = (product * root_scale).astype(jnp.bfloat16)
            for core in range(2):
                part = scaled[:, core * evecs : (core + 1) * evecs].reshape(rows, evecs, evecs)
                table[pl.ds((base + core) * sinks + block * rows, rows)] = part
    all_sent(send_sem.at[0])

    def half_sum(top):
        def graph_step(block, total):
            start = UNROLL * block
            left = [table[graph_ref[0, start + graph], top : top + HALF] for graph in range(UNROLL)]
            right = [table[graph_ref[1, start + graph]] for graph in range(UNROLL)]
            return total + jnp.dot(
                jnp.concatenate(left, axis=1),
                jnp.concatenate(right, axis=0),
                preferred_element_type=jnp.float32,
            )

        return lax.fori_loop(
            0, graphs // UNROLL, graph_step, jnp.zeros((HALF, evecs), jnp.float32)
        )

    def edge_copy(step, hop, part, semaphore):
        owner = flip(me, step)
        rows = edges.at[owner, pl.ds(part * HALF, HALF)]
        return pltpu.make_async_remote_copy(
            src_ref=rows,
            dst_ref=rows,
            send_sem=send_sem.at[1],
            recv_sem=semaphore,
            **at(flip(me, hop)),
        )

    def pass_on(step, part):
        for child in SENDS:
            hop = HOP[child]
            if child ^ hop == step:
                semaphore = edge_recv_sem.at[part, child // 2 if hop != 1 else 0]
                edge_copy(step, hop, part, semaphore).start()

    parts = evecs // HALF
    for part in range(parts):
        with jax.named_scope(f"graphs{part}"):
            piece = (half_sum(part * HALF) * edge_scale).astype(jnp.bfloat16)
            edges[me, part * HALF : (part + 1) * HALF] = piece
        pass_on(0, part)
        edge_out[0, part * HALF : (part + 1) * HALF] = piece
    for part in range(parts):
        for step in WAITS:
            with jax.named_scope(f"gather{part}_{step}"):
                edge_copy(step, 1, part, edge_recv_sem.at[part, step // 2]).wait_recv()
            pass_on(step, part)
    with jax.named_scope("partner"):
        by_partner = sum(HOP[child] == 1 for child in SENDS)
        for part in range(parts):
            rows = edges.at[pl.ds(0, by_partner), pl.ds(part * HALF, HALF)]
            pltpu.make_async_remote_copy(
                src_ref=rows,
                dst_ref=rows,
                send_sem=send_sem.at[1],
                recv_sem=edge_recv_sem.at[part, 0],
                **at(flip(me, 1)),
            ).wait_recv()
    with jax.named_scope("pairs"):
        for pair in range(product_out.shape[0]):
            product = jnp.dot(
                edges[pair_ref[0, pair]],
                edges[pair_ref[1, pair]],
                preferred_element_type=jnp.float32,
            )
            product_out[pair] = (product * root_scale).astype(jnp.bfloat16)
    all_sent(send_sem.at[1])


def store_kernel(edge_in, product_in, edge_out, product_out, store_sem):
    edge_copy = pltpu.make_async_copy(edge_in, edge_out, store_sem.at[0])
    product_copy = pltpu.make_async_copy(product_in, product_out, store_sem.at[1])
    edge_copy.start()
    product_copy.start()
    edge_copy.wait()
    product_copy.wait()


def fused_shards(
    n,
    source_slabs,
    sink_slabs,
    perambulators,
    send_pick,
    graph_slot,
    graph_sink,
    graph_count,
    pair_list,
):
    sinks, evecs, _ = sink_slabs.shape
    graphs = graph_slot.shape[1]
    pairs = pair_list.shape[0]
    vmem = pl.BlockSpec(memory_space=pltpu.VMEM)
    hbm = pl.BlockSpec(memory_space=pltpu.HBM)
    slab = (evecs, evecs)
    held = pl.pallas_call(
        functools.partial(fused_kernel, n, graphs),
        out_shape=(
            pltpu.VMEM((1, *slab), jnp.bfloat16),
            pltpu.VMEM((pairs, *slab), jnp.bfloat16),
        ),
        in_specs=[hbm] * 8,
        out_specs=(vmem, vmem),
        scratch_shapes=[
            pltpu.VMEM((n, *slab), jnp.bfloat16),
            pltpu.VMEM((n, *slab), jnp.bfloat16),
            pltpu.VMEM((n, *slab), jnp.bfloat16),
            pltpu.VMEM((n * sinks + 1, *slab), jnp.bfloat16),
            pltpu.VMEM((2, graphs), jnp.int32),
            pltpu.VMEM((2, graphs), jnp.int32),
            pltpu.VMEM((2, graphs), jnp.int32),
            pltpu.SMEM(send_pick.shape, jnp.int32),
            pltpu.SMEM((1,), jnp.int32),
            pltpu.SMEM((2, pairs), jnp.int32),
            pltpu.SMEM((2, graphs), jnp.int32),
            pltpu.VMEM(perambulators.shape, jnp.bfloat16),
            pltpu.VMEM(source_slabs.shape, jnp.bfloat16),
            pltpu.VMEM(sink_slabs.shape, jnp.bfloat16),
            pltpu.SemaphoreType.DMA((9,)),
            pltpu.SemaphoreType.DMA((2,)),
            pltpu.SemaphoreType.DMA((n // 2,)),
            pltpu.SemaphoreType.DMA((evecs // HALF, n // 2)),
        ],
        compiler_params=pltpu.CompilerParams(
            collective_id=0, has_side_effects=True
        ),
        name="contraction",
    )(
        send_pick,
        graph_slot[0].T,
        graph_sink[0].T,
        graph_count,
        pair_list.T,
        perambulators,
        source_slabs,
        sink_slabs,
    )
    return pl.pallas_call(
        store_kernel,
        out_shape=tuple(jax.ShapeDtypeStruct(part.shape, part.dtype) for part in held),
        in_specs=[vmem, vmem],
        out_specs=(hbm, hbm),
        scratch_shapes=[pltpu.SemaphoreType.DMA((2,))],
        compiler_params=pltpu.CompilerParams(vmem_limit_bytes=1024 * 1024),
        name="store",
    )(*(pltpu.with_memory_space_constraint(part, pltpu.VMEM) for part in held))


def shards(readers, source_slabs, sink_slabs, perambulators, *tables):
    slabs = sink_slabs.shape[0]
    graphs = tables[1].shape[1]
    power = readers & (readers - 1) == 0 and readers % 4 == 0
    if power and readers * slabs <= 2 * graphs and graphs % UNROLL == 0 and slabs % 4 == 0:
        return fused_shards(readers, source_slabs, sink_slabs, perambulators, *tables)
    return looped_shards(source_slabs, sink_slabs, perambulators, *tables)


def solution(mesh):
    return jax.shard_map(
        functools.partial(shards, mesh.shape["had"]),
        mesh=mesh,
        in_specs=(
            P(("grp", "had"), None, None),
            P(("grp", "had"), None, None),
            P("grp", None, None, None),
            P(("grp", "had"), None),
            P(("grp", "had"), None, None),
            P(("grp", "had"), None, None),
            P(("grp", "had")),
            P(("grp", "had"), None),
        ),
        out_specs=(P(("grp", "had"), None, None), P(("grp", "had"), None, None)),
        check_vma=False,
    )
```

```python
import functools
import math

import jax
import jax.numpy as jnp
from jax import lax
from jax.experimental import pallas as pl
from jax.experimental.pallas import tpu as pltpu
from jax.sharding import PartitionSpec as P


def looped_shards(
    source_slabs,
    sink_slabs,
    perambulators,
    send_pick,
    graph_slot,
    graph_sink,
    graph_count,
    pair_list,
):
    my_index = lax.axis_index("had")
    evecs = source_slabs.shape[1]
    per_device = source_slabs.shape[0]
    root_scale = 1.0 / math.sqrt(evecs)
    edge_scale = 1.0 / math.sqrt(evecs * graph_slot.shape[1])
    timeslice = my_index * per_device // evecs
    local_peram = lax.dynamic_index_in_dim(perambulators, timeslice, 0, keepdims=False)
    first_turn = jnp.einsum(
        "xa,jab->xjb", local_peram[0], source_slabs, preferred_element_type=jnp.float32
    ).astype(jnp.bfloat16)
    pick_row = send_pick[0]
    second_turn = jnp.einsum(
        "xjb,yb->xjy", first_turn, local_peram[1], preferred_element_type=jnp.float32
    ).astype(jnp.bfloat16)
    outgoing = jnp.take(second_turn, pick_row, axis=1)
    received = lax.all_to_all(outgoing, "had", split_axis=1, concat_axis=1, tiled=True)
    graph_rows = graph_slot.shape[1]
    block_width = min(64, graph_rows)
    slot_table = graph_slot[0]
    sink_table = graph_sink[0]
    graph_total = graph_count[0]

    def factor(slots, sinks):
        gathered = jnp.take(received, slots, axis=1)
        resident = jnp.take(sink_slabs, sinks, axis=0)
        product = jnp.einsum("gxb,agb->gxa", resident, gathered, preferred_element_type=jnp.float32)
        return (product * root_scale).astype(jnp.bfloat16)

    def accumulate(block_index, running_sum):
        offset = block_index * block_width
        slots = lax.dynamic_slice_in_dim(slot_table, offset, block_width, 0)
        sinks = lax.dynamic_slice_in_dim(sink_table, offset, block_width, 0)
        is_valid = (offset + jnp.arange(block_width, dtype=jnp.int32) < graph_total).astype(
            jnp.bfloat16
        )
        left_side = factor(slots[:, 0], sinks[:, 0]) * is_valid[:, None, None]
        right_side = factor(slots[:, 1], sinks[:, 1])
        return running_sum + jnp.einsum(
            "gxa,gay->xy", left_side, right_side, preferred_element_type=jnp.float32
        )

    block_count = (graph_total + block_width - 1) // block_width
    summed = lax.fori_loop(0, block_count, accumulate, jnp.zeros((evecs, evecs), jnp.float32))
    edge_local = (summed * edge_scale).astype(jnp.bfloat16)[None]
    left_ids = pair_list[:, 0]
    right_ids = pair_list[:, 1]
    shard_rows = lax.all_gather(edge_local, "had", axis=0, tiled=True)
    row_ids = jnp.arange(shard_rows.shape[0], dtype=jnp.int32)
    left_select = (left_ids[:, None] == row_ids[None, :]).astype(jnp.bfloat16)
    right_select = (right_ids[:, None] == row_ids[None, :]).astype(jnp.bfloat16)
    left_part = jnp.einsum(
        "pn,nxy->pxy", left_select, shard_rows, preferred_element_type=jnp.float32
    )
    right_part = jnp.einsum(
        "pn,nxy->pxy", right_select, shard_rows, preferred_element_type=jnp.float32
    )
    left_edges = left_part.astype(jnp.bfloat16)
    right_edges = right_part.astype(jnp.bfloat16)
    product = jnp.einsum(
        "pxa,pay->pxy", left_edges, right_edges, preferred_element_type=jnp.float32
    )
    pair_products = (product * root_scale).astype(jnp.bfloat16)
    return (edge_local, pair_products)


NT = (((1,), (1,)), ((), ()))
UNROLL = 256
HALF = 64


def flip(index, step):
    flipped = index
    bit = 1
    while bit <= step:
        if step & bit:
            flipped = flipped + bit * (1 - 2 * (index // bit % 2))
        bit *= 2
    return flipped


def fused_kernel(
    n,
    graphs,
    pick_in,
    slot_in,
    graph_sink_in,
    count_in,
    pair_in,
    peram_in,
    source_in,
    sink_in,
    edge_out,
    product_out,
    edges,
    outgoing,
    received,
    table,
    slot_ref,
    graph_sink_ref,
    index_ref,
    pick_ref,
    count_ref,
    pair_ref,
    graph_ref,
    peram_ref,
    source_ref,
    sink_ref,
    load_sem,
    send_sem,
    recv_sem,
    edge_recv_sem,
):
    me = lax.axis_index("had")
    per_device, evecs, _ = source_ref.shape
    root_scale = 1.0 / math.sqrt(evecs)
    edge_scale = root_scale**2 / math.sqrt(evecs * graphs)
    sinks = sink_ref.shape[0]

    def at(peer):
        return dict(device_id={"had": peer}, device_id_type=pl.DeviceIdType.MESH)

    barrier = pltpu.get_barrier_semaphore()
    for step in range(n - 1, 0, -1):
        pl.semaphore_signal(barrier, inc=1, **at(flip(me, step)))

    loads = {}
    for name, source, target in (
        ("pick", pick_in, pick_ref),
        ("peram", peram_in, peram_ref),
        ("source", source_in, source_ref),
        ("slot", slot_in, slot_ref),
        ("graph_sink", graph_sink_in, graph_sink_ref),
        ("count", count_in, count_ref),
        ("sink", sink_in, sink_ref),
        ("pair", pair_in, pair_ref),
    ):
        loads[name] = pltpu.make_async_copy(source, target, load_sem.at[len(loads)])
        loads[name].start()
    with jax.named_scope("load"):
        for name in ("pick", "peram", "source"):
            loads[name].wait()

    timeslice = me * per_device // evecs
    first = peram_ref[timeslice, 0]
    second = peram_ref[timeslice, 1]
    chips = n // 2
    levels = chips // 2
    chip, core = me // 2, me % 2
    level, row = chip // 2, chip % 2
    upper = chip // levels

    def across(distance, other_row):
        far = (1 - upper) * (chips // 2 - 1 - distance) + upper * distance
        return 2 * far + row + other_row * (1 - 2 * row)

    in_half = level % (levels // 2)
    inner = upper * (1 - in_half) + (1 - upper) * in_half

    def through(distance):
        return [
            (2 * across(distance, other) + side, levels + 2 * other + in_half)
            for side in range(2)
            for other in range(2)
        ]

    near = [flip(chip, step) for step in range(levels)]
    peers = through(0)
    for step in range(1, levels):
        peers += [(2 * near[step] + 1 - core, step), (2 * near[step] + core, step)]
    peers += through(1)
    peers += [(2 * chip + 1 - core, 0), (me, None)]

    def rotate(targets):
        halves = []
        for peer, _ in targets:
            slab = source_ref[pick_ref[0, peer]]
            half = jnp.dot(first, slab, preferred_element_type=jnp.float32)
            halves.append(half.astype(jnp.bfloat16))
        for (peer, _), half in zip(targets, halves):
            turned = lax.dot_general(half, second, NT, preferred_element_type=jnp.float32)
            target = received if peer is me else outgoing
            target[peer] = turned.astype(jnp.bfloat16)

    def send(targets):
        for peer, place in targets:
            if place is not None:
                pltpu.make_async_remote_copy(
                    src_ref=outgoing.at[peer],
                    dst_ref=received.at[me],
                    send_sem=send_sem.at[0],
                    recv_sem=recv_sem.at[place],
                    **at(peer),
                ).start()

    def arrival(buffer, semaphore):
        return pltpu.make_async_remote_copy(
            src_ref=buffer,
            dst_ref=buffer,
            send_sem=send_sem.at[0],
            recv_sem=semaphore,
            **at(2 * chip + 1 - core),
        )

    def all_sent(semaphore, slabs):
        pltpu.make_async_remote_copy(
            src_ref=table.at[pl.ds(0, slabs)],
            dst_ref=table.at[pl.ds(0, slabs)],
            send_sem=semaphore,
            recv_sem=recv_sem.at[0],
            **at(2 * chip + 1 - core),
        ).wait_send()

    group = 4
    for at_group in range(0, n, group):
        targets = peers[at_group : at_group + group]
        with jax.named_scope(f"rotate{at_group}"):
            rotate(targets)
        if at_group == 0:
            with jax.named_scope("meet"):
                pl.semaphore_wait(barrier, n - 1)
        send(targets)

    with jax.named_scope("index"):
        for name in ("slot", "graph_sink", "count"):
            loads[name].wait()
        graph_ids = lax.broadcasted_iota(jnp.int32, slot_ref.shape, 1)
        index_ref[...] = jnp.where(
            graph_ids < count_ref[0], slot_ref[...] * sinks + graph_sink_ref[...], n * sinks
        )
        index_load = pltpu.make_async_copy(index_ref, graph_ref, load_sem.at[len(loads)])
        index_load.start()
        table[n * sinks] = jnp.zeros((evecs, evecs), jnp.bfloat16)
        rows = 4
        loads["sink"].wait()
        loads["pair"].wait()
        index_load.wait()


    def source(place, other):
        return 2 * ((1 - upper) * (levels // 2) + place) + row + other * (1 - 2 * row)

    from_near = [(near[step], step) for step in range(levels)]
    from_far = [
        (source(place, other), levels + 2 * other + place)
        for other in range(2)
        for place in (upper, 1 - upper)
    ]
    order_inner = from_near + from_far
    order_outer = from_near[:2] + from_far + from_near[2:]
    for place, (when_inner, when_outer) in enumerate(zip(order_inner, order_outer)):
        owner, semaphore = (
            inner * one + (1 - inner) * two for one, two in zip(when_inner, when_outer)
        )
        with jax.named_scope(f"arrive{place}"):
            landed = received.at[pl.ds(0, 2)] if place else received.at[0]
            arrival(landed, recv_sem.at[semaphore]).wait_recv()
        both = received[pl.ds(2 * owner, 2)].reshape(2 * evecs, evecs)
        for block in range(sinks // rows):
            left = sink_ref[block * rows : (block + 1) * rows].reshape(rows * evecs, evecs)
            product = lax.dot_general(left, both, NT, preferred_element_type=jnp.float32)
            factors = product.astype(jnp.bfloat16)
            for side in range(2):
                part = factors[:, side * evecs : (side + 1) * evecs].reshape(rows, evecs, evecs)
                table[pl.ds((2 * owner + side) * sinks + block * rows, rows)] = part
    all_sent(send_sem.at[0], n - 1)

    def half_sum(top):
        def graph_step(block, total):
            start = UNROLL * block
            left = [table[graph_ref[0, start + graph], top : top + HALF] for graph in range(UNROLL)]
            right = [table[graph_ref[1, start + graph]] for graph in range(UNROLL)]
            return total + jnp.dot(
                jnp.concatenate(left, axis=1),
                jnp.concatenate(right, axis=0),
                preferred_element_type=jnp.float32,
            )

        return lax.fori_loop(
            0, graphs // UNROLL, graph_step, jnp.zeros((HALF, evecs), jnp.float32)
        )

    def edge_send(owners, count, part, peer, semaphore):
        rows_of = edges.at[pl.ds(owners, count), pl.ds(part * HALF, HALF)]
        pltpu.make_async_remote_copy(
            src_ref=rows_of,
            dst_ref=rows_of,
            send_sem=send_sem.at[1],
            recv_sem=semaphore,
            **at(peer),
        ).start()

    def edge_landed(owners, count, part, semaphore):
        rows_of = edges.at[pl.ds(owners, count), pl.ds(part * HALF, HALF)]
        arrival(rows_of, semaphore).wait_recv()

    my_place = 2 * (chip * (1 - upper) + (chips - 1 - chip) * upper) + upper

    def other_chip(turn):
        place = turn + (turn + chips - my_place) // chips
        return place % 2 * (chips - 1) + (1 - 2 * (place % 2)) * (place // 2)

    def spread(part):
        landing = edge_recv_sem.at[part * (1 + inner)]
        for turn in range(chips - 1):
            edge_send(me, 1, part, 2 * other_chip(turn) + 1, landing)

        @pl.when(core == 1)
        def to_first():
            edge_send(me, 1, part, me - 1, edge_recv_sem.at[0])

        @pl.when(core == 0)
        def to_second():
            edge_send(me, 1, part, me + 1, landing)

    for part in range(2):
        with jax.named_scope(f"graphs{part}"):
            piece = (half_sum(part * HALF) * edge_scale).astype(jnp.bfloat16)
            edges[me, part * HALF : (part + 1) * HALF] = piece
        spread(part)
        edge_out[0, part * HALF : (part + 1) * HALF] = piece

    def relay(stages):
        turn = 0
        for part, semaphore, count in stages:
            with jax.named_scope(f"gather{semaphore}"):
                edge_landed(0, count, part, edge_recv_sem.at[semaphore])
            for place in range(turn, turn + count // 2):
                edge_send(2 * other_chip(place), 2, part, me - 1, edge_recv_sem.at[0])
            turn = (turn + count // 2) % (chips - 1)

    @pl.when((core == 1) & (inner == 1))
    def relay_inner():
        relay([(0, 0, n - 1), (1, 1, chips), (1, 2, chips - 1)])

    @pl.when((core == 1) & (inner == 0))
    def relay_outer():
        relay([(0, 0, n - 1), (1, 1, chips - 1), (1, 2, chips)])

    @pl.when(core == 0)
    def take_over():
        with jax.named_scope("partner0"):
            arrival(edges.at[pl.ds(0, n - 1)], edge_recv_sem.at[0]).wait_recv()

    with jax.named_scope("pairs"):
        for pair in range(product_out.shape[0]):
            product = jnp.dot(
                edges[pair_ref[0, pair]],
                edges[pair_ref[1, pair]],
                preferred_element_type=jnp.float32,
            )
            product_out[pair] = (product * root_scale).astype(jnp.bfloat16)

    @pl.when(core == 1)
    def sent_by_second():
        all_sent(send_sem.at[1], 3 * chips - 2)

    @pl.when(core == 0)
    def sent_by_first():
        all_sent(send_sem.at[1], chips)


def store_kernel(edge_in, product_in, edge_out, product_out, store_sem):
    edge_copy = pltpu.make_async_copy(edge_in, edge_out, store_sem.at[0])
    product_copy = pltpu.make_async_copy(product_in, product_out, store_sem.at[1])
    edge_copy.start()
    product_copy.start()
    edge_copy.wait()
    product_copy.wait()


def fused_shards(
    n,
    source_slabs,
    sink_slabs,
    perambulators,
    send_pick,
    graph_slot,
    graph_sink,
    graph_count,
    pair_list,
):
    sinks, evecs, _ = sink_slabs.shape
    graphs = graph_slot.shape[1]
    pairs = pair_list.shape[0]
    vmem = pl.BlockSpec(memory_space=pltpu.VMEM)
    hbm = pl.BlockSpec(memory_space=pltpu.HBM)
    slab = (evecs, evecs)
    held = pl.pallas_call(
        functools.partial(fused_kernel, n, graphs),
        out_shape=(
            pltpu.VMEM((1, *slab), jnp.bfloat16),
            pltpu.VMEM((pairs, *slab), jnp.bfloat16),
        ),
        in_specs=[hbm] * 8,
        out_specs=(vmem, vmem),
        scratch_shapes=[
            pltpu.VMEM((n, *slab), jnp.bfloat16),
            pltpu.VMEM((n, *slab), jnp.bfloat16),
            pltpu.VMEM((n, *slab), jnp.bfloat16),
            pltpu.VMEM((n * sinks + 1, *slab), jnp.bfloat16),
            pltpu.VMEM((2, graphs), jnp.int32),
            pltpu.VMEM((2, graphs), jnp.int32),
            pltpu.VMEM((2, graphs), jnp.int32),
            pltpu.SMEM(send_pick.shape, jnp.int32),
            pltpu.SMEM((1,), jnp.int32),
            pltpu.SMEM((2, pairs), jnp.int32),
            pltpu.SMEM((2, graphs), jnp.int32),
            pltpu.VMEM(perambulators.shape, jnp.bfloat16),
            pltpu.VMEM(source_slabs.shape, jnp.bfloat16),
            pltpu.VMEM(sink_slabs.shape, jnp.bfloat16),
            pltpu.SemaphoreType.DMA((9,)),
            pltpu.SemaphoreType.DMA((2,)),
            pltpu.SemaphoreType.DMA((n // 2,)),
            pltpu.SemaphoreType.DMA((3,)),
        ],
        compiler_params=pltpu.CompilerParams(
            collective_id=0, has_side_effects=True
        ),
        name="contraction",
    )(
        send_pick,
        graph_slot[0].T,
        graph_sink[0].T,
        graph_count,
        pair_list.T,
        perambulators,
        source_slabs,
        sink_slabs,
    )
    return pl.pallas_call(
        store_kernel,
        out_shape=tuple(jax.ShapeDtypeStruct(part.shape, part.dtype) for part in held),
        in_specs=[vmem, vmem],
        out_specs=(hbm, hbm),
        scratch_shapes=[pltpu.SemaphoreType.DMA((2,))],
        compiler_params=pltpu.CompilerParams(vmem_limit_bytes=1024 * 1024),
        name="store",
    )(*(pltpu.with_memory_space_constraint(part, pltpu.VMEM) for part in held))


def shards(readers, source_slabs, sink_slabs, perambulators, *tables):
    slabs = sink_slabs.shape[0]
    graphs = tables[1].shape[1]
    power = readers & (readers - 1) == 0 and readers // 8 == 2
    if power and readers * slabs <= 2 * graphs and graphs % UNROLL == 0 and slabs % 4 == 0 and sink_slabs.shape[1] == 2 * HALF:
        return fused_shards(readers, source_slabs, sink_slabs, perambulators, *tables)
    return looped_shards(source_slabs, sink_slabs, perambulators, *tables)


def solution(mesh):
    return jax.shard_map(
        functools.partial(shards, mesh.shape["had"]),
        mesh=mesh,
        in_specs=(
            P(("grp", "had"), None, None),
            P(("grp", "had"), None, None),
            P("grp", None, None, None),
            P(("grp", "had"), None),
            P(("grp", "had"), None, None),
            P(("grp", "had"), None, None),
            P(("grp", "had")),
            P(("grp", "had"), None),
        ),
        out_specs=(P(("grp", "had"), None, None), P(("grp", "had"), None, None)),
        check_vma=False,
    )
```

```python
import functools
import math

import jax
import jax.numpy as jnp
from jax import lax
from jax.experimental import pallas as pl
from jax.experimental.pallas import tpu as pltpu
from jax.sharding import PartitionSpec as P


def looped_shards(
    source_slabs,
    sink_slabs,
    perambulators,
    send_pick,
    graph_slot,
    graph_sink,
    graph_count,
    pair_list,
):
    my_index = lax.axis_index("had")
    evecs = source_slabs.shape[1]
    per_device = source_slabs.shape[0]
    root_scale = 1.0 / math.sqrt(evecs)
    edge_scale = 1.0 / math.sqrt(evecs * graph_slot.shape[1])
    timeslice = my_index * per_device // evecs
    local_peram = lax.dynamic_index_in_dim(perambulators, timeslice, 0, keepdims=False)
    first_turn = jnp.einsum(
        "xa,jab->xjb", local_peram[0], source_slabs, preferred_element_type=jnp.float32
    ).astype(jnp.bfloat16)
    pick_row = send_pick[0]
    second_turn = jnp.einsum(
        "xjb,yb->xjy", first_turn, local_peram[1], preferred_element_type=jnp.float32
    ).astype(jnp.bfloat16)
    outgoing = jnp.take(second_turn, pick_row, axis=1)
    received = lax.all_to_all(outgoing, "had", split_axis=1, concat_axis=1, tiled=True)
    graph_rows = graph_slot.shape[1]
    block_width = min(64, graph_rows)
    slot_table = graph_slot[0]
    sink_table = graph_sink[0]
    graph_total = graph_count[0]

    def factor(slots, sinks):
        gathered = jnp.take(received, slots, axis=1)
        resident = jnp.take(sink_slabs, sinks, axis=0)
        product = jnp.einsum("gxb,agb->gxa", resident, gathered, preferred_element_type=jnp.float32)
        return (product * root_scale).astype(jnp.bfloat16)

    def accumulate(block_index, running_sum):
        offset = block_index * block_width
        slots = lax.dynamic_slice_in_dim(slot_table, offset, block_width, 0)
        sinks = lax.dynamic_slice_in_dim(sink_table, offset, block_width, 0)
        is_valid = (offset + jnp.arange(block_width, dtype=jnp.int32) < graph_total).astype(
            jnp.bfloat16
        )
        left_side = factor(slots[:, 0], sinks[:, 0]) * is_valid[:, None, None]
        right_side = factor(slots[:, 1], sinks[:, 1])
        return running_sum + jnp.einsum(
            "gxa,gay->xy", left_side, right_side, preferred_element_type=jnp.float32
        )

    block_count = (graph_total + block_width - 1) // block_width
    summed = lax.fori_loop(0, block_count, accumulate, jnp.zeros((evecs, evecs), jnp.float32))
    edge_local = (summed * edge_scale).astype(jnp.bfloat16)[None]
    left_ids = pair_list[:, 0]
    right_ids = pair_list[:, 1]
    shard_rows = lax.all_gather(edge_local, "had", axis=0, tiled=True)
    row_ids = jnp.arange(shard_rows.shape[0], dtype=jnp.int32)
    left_select = (left_ids[:, None] == row_ids[None, :]).astype(jnp.bfloat16)
    right_select = (right_ids[:, None] == row_ids[None, :]).astype(jnp.bfloat16)
    left_part = jnp.einsum(
        "pn,nxy->pxy", left_select, shard_rows, preferred_element_type=jnp.float32
    )
    right_part = jnp.einsum(
        "pn,nxy->pxy", right_select, shard_rows, preferred_element_type=jnp.float32
    )
    left_edges = left_part.astype(jnp.bfloat16)
    right_edges = right_part.astype(jnp.bfloat16)
    product = jnp.einsum(
        "pxa,pay->pxy", left_edges, right_edges, preferred_element_type=jnp.float32
    )
    pair_products = (product * root_scale).astype(jnp.bfloat16)
    return (edge_local, pair_products)


NT = (((1,), (1,)), ((), ()))
LANES = 128
ROUNDS = 2


def column(values):
    return jnp.concatenate(
        [
            jnp.broadcast_to(values[:, start : start + LANES], (LANES, LANES)).T
            for start in range(0, values.shape[1], LANES)
        ],
        axis=0,
    )


def pair_up(left, right, tables, entries):
    graphs = left.shape[1]
    left_column = column(left)
    turns = lax.broadcasted_iota(jnp.int32, (graphs, LANES), 0)
    lanes = lax.broadcasted_iota(jnp.int32, (graphs, LANES), 1)
    ranks = []
    for start in range(0, graphs, LANES):
        same = left_column == left[:, start : start + LANES]
        ahead = jnp.where(same & (turns < lanes + start), 1, 0)
        ranks.append(jnp.sum(ahead, axis=0, keepdims=True))
    rank = jnp.concatenate(ranks, axis=1)
    opens = jnp.where(column(rank) % 2 == 0, left_column, tables + 1)
    keys = []
    for start in range(0, graphs, LANES):
        below = jnp.where(opens < left[:, start : start + LANES], 2, 0)
        keys.append(jnp.sum(below, axis=0, keepdims=True) + rank[:, start : start + LANES])
    key_column = column(jnp.concatenate(keys, axis=1))
    right_column = column(right) + 1
    shift = 2 * tables
    packed = left_column * shift + right_column
    rows = ([], [], [])
    for start in range(0, entries, LANES):
        here = key_column - 2 * (lanes + start)
        even = jnp.sum(jnp.where(here == 0, packed, 0), axis=0, keepdims=True)
        odd = jnp.sum(jnp.where(here == 1, right_column, 0), axis=0, keepdims=True)
        used = even > 0
        rows[0].append(jnp.where(used, even // shift, tables))
        rows[1].append(jnp.where(used, even % shift - 1, tables))
        rows[2].append(jnp.where(odd > 0, odd - 1, tables))
    return [jnp.concatenate(row, axis=1) for row in rows]


def flip(index, step):
    flipped = index
    bit = 1
    while bit <= step:
        if step & bit:
            flipped = flipped + bit * (1 - 2 * (index // bit % 2))
        bit *= 2
    return flipped


def fused_kernel(
    n,
    graphs,
    pick_in,
    slot_in,
    graph_sink_in,
    count_in,
    pair_in,
    peram_in,
    source_in,
    sink_in,
    edge_out,
    product_out,
    edges,
    outgoing,
    received,
    table,
    slot_ref,
    graph_sink_ref,
    index_ref,
    pick_ref,
    count_ref,
    pair_ref,
    graph_ref,
    peram_ref,
    source_ref,
    sink_ref,
    load_sem,
    send_sem,
    recv_sem,
    edge_recv_sem,
):
    me = lax.axis_index("had")
    per_device, evecs, _ = source_ref.shape
    root_scale = 1.0 / math.sqrt(evecs)
    edge_scale = 1.0 / math.sqrt(evecs * graphs)
    sinks = sink_ref.shape[0]
    entries = graph_ref.shape[1]
    unroll = entries // ROUNDS

    def at(peer):
        return dict(device_id={"had": peer}, device_id_type=pl.DeviceIdType.MESH)

    barrier = pltpu.get_barrier_semaphore()
    for step in range(n - 1, 0, -1):
        pl.semaphore_signal(barrier, inc=1, **at(flip(me, step)))

    loads = {}
    for name, source, target in (
        ("pick", pick_in, pick_ref),
        ("peram", peram_in, peram_ref),
        ("source", source_in, source_ref),
        ("slot", slot_in, slot_ref),
        ("graph_sink", graph_sink_in, graph_sink_ref),
        ("count", count_in, count_ref),
        ("sink", sink_in, sink_ref),
        ("pair", pair_in, pair_ref),
    ):
        loads[name] = pltpu.make_async_copy(source, target, load_sem.at[len(loads)])
        loads[name].start()
    with jax.named_scope("load"):
        for name in ("pick", "peram", "source"):
            loads[name].wait()

    timeslice = me * per_device // evecs
    first = peram_ref[timeslice, 0]
    second = peram_ref[timeslice, 1]
    chips = n // 2
    levels = chips // 2
    chip, core = me // 2, me % 2
    level, row = chip // 2, chip % 2
    upper = chip // levels

    def across(distance, other_row):
        far = (1 - upper) * (chips // 2 - 1 - distance) + upper * distance
        return 2 * far + row + other_row * (1 - 2 * row)

    in_half = level % (levels // 2)
    inner = upper * (1 - in_half) + (1 - upper) * in_half

    def through(distance):
        return [
            (2 * across(distance, other) + side, levels + 2 * other + in_half)
            for side in range(2)
            for other in range(2)
        ]

    near = [flip(chip, step) for step in range(levels)]
    peers = through(0)
    for step in range(1, levels):
        peers += [(2 * near[step] + 1 - core, step), (2 * near[step] + core, step)]
    peers += through(1)
    peers += [(2 * chip + 1 - core, 0), (me, None)]

    def rotate(targets):
        halves = []
        for peer, _ in targets:
            slab = source_ref[pick_ref[0, peer]]
            half = jnp.dot(first, slab, preferred_element_type=jnp.float32)
            halves.append(half.astype(jnp.bfloat16))
        for (peer, _), half in zip(targets, halves):
            turned = lax.dot_general(half, second, NT, preferred_element_type=jnp.float32)
            target = received if peer is me else outgoing
            target[peer] = turned.astype(jnp.bfloat16)

    def send(targets):
        for peer, place in targets:
            if place is not None:
                pltpu.make_async_remote_copy(
                    src_ref=outgoing.at[peer],
                    dst_ref=received.at[me],
                    send_sem=send_sem.at[0],
                    recv_sem=recv_sem.at[place],
                    **at(peer),
                ).start()

    def arrival(buffer, semaphore):
        return pltpu.make_async_remote_copy(
            src_ref=buffer,
            dst_ref=buffer,
            send_sem=send_sem.at[0],
            recv_sem=semaphore,
            **at(2 * chip + 1 - core),
        )

    def all_sent(semaphore, slabs):
        pltpu.make_async_remote_copy(
            src_ref=table.at[pl.ds(0, slabs)],
            dst_ref=table.at[pl.ds(0, slabs)],
            send_sem=semaphore,
            recv_sem=recv_sem.at[0],
            **at(2 * chip + 1 - core),
        ).wait_send()

    group = 4
    for at_group in range(0, n, group):
        targets = peers[at_group : at_group + group]
        with jax.named_scope(f"rotate{at_group}"):
            rotate(targets)
        if at_group == 0:
            with jax.named_scope("meet"):
                pl.semaphore_wait(barrier, n - 1)
        send(targets)

    with jax.named_scope("index"):
        for name in ("slot", "graph_sink", "count"):
            loads[name].wait()
        graph_ids = lax.broadcasted_iota(jnp.int32, slot_ref.shape, 1)
        places = slot_ref[...] * sinks + graph_sink_ref[...]
        left_ids = jnp.where(graph_ids[:1] < count_ref[0], places[:1], n * sinks)
        for place, ids in enumerate(pair_up(left_ids, places[1:], n * sinks, entries)):
            index_ref[place : place + 1] = ids
        index_load = pltpu.make_async_copy(index_ref, graph_ref, load_sem.at[len(loads)])
        index_load.start()
        table[n * sinks] = jnp.zeros((evecs, evecs), jnp.bfloat16)
        rows = 4
        loads["sink"].wait()
        loads["pair"].wait()
        index_load.wait()


    def source(place, other):
        return 2 * ((1 - upper) * (levels // 2) + place) + row + other * (1 - 2 * row)

    from_near = [(near[step], step) for step in range(levels)]
    from_far = [
        (source(place, other), levels + 2 * other + place)
        for other in range(2)
        for place in (upper, 1 - upper)
    ]
    def fill(units, skip=0):
        places = [
            [inner * one + (1 - inner) * two for one, two in zip(*unit)] for unit in units
        ]
        for owner, semaphore in places[skip:]:
            landed = received.at[pl.ds(0, 2)]
            arrival(landed, recv_sem.at[semaphore]).wait_recv()
        for block in range(sinks // rows):
            left = sink_ref[block * rows : (block + 1) * rows].reshape(rows * evecs, evecs)
            for owner, _ in places:
                both = received[pl.ds(2 * owner, 2)].reshape(2 * evecs, evecs)
                product = lax.dot_general(left, both, NT, preferred_element_type=jnp.float32)
                factors = (product * root_scale).astype(jnp.bfloat16)
                for side in range(2):
                    part = factors[:, side * evecs : (side + 1) * evecs].reshape(rows, evecs, evecs)
                    table[pl.ds((2 * owner + side) * sinks + block * rows, rows)] = part

    with jax.named_scope("arrive0"):
        arrival(received.at[0], recv_sem.at[0]).wait_recv()
    order_inner = from_near + from_far
    order_outer = from_near[:2] + from_far + from_near[2:]
    units = list(zip(order_inner, order_outer))
    fill(units[:1], skip=1)
    with jax.named_scope("fill1"):
        fill(units[1:2])
    with jax.named_scope("fill2"):
        fill(units[2:3])
    with jax.named_scope("fill3"):
        fill(units[3:4])
    with jax.named_scope("fill4"):
        fill(units[4:6])
    with jax.named_scope("fill6"):
        fill(units[6:8])
    all_sent(send_sem.at[0], n - 1)

    def graph_step(block, total):
        start = unroll * block
        left = [table[graph_ref[0, start + entry]] for entry in range(unroll)]
        right = [
            jnp.concatenate([table[graph_ref[side, start + entry]] for side in (1, 2)], axis=1)
            for entry in range(unroll)
        ]
        both = jnp.dot(
            jnp.concatenate(left, axis=1),
            jnp.concatenate(right, axis=0),
            preferred_element_type=jnp.float32,
        )
        return total + both[:, :evecs] + both[:, evecs:]

    def edge_send(owners, count, peer, semaphore):
        pltpu.make_async_remote_copy(
            src_ref=edges.at[pl.ds(owners, count)],
            dst_ref=edges.at[pl.ds(owners, count)],
            send_sem=send_sem.at[1],
            recv_sem=edge_recv_sem.at[semaphore],
            **at(peer),
        ).start()

    my_place = 2 * (chip * (1 - upper) + (chips - 1 - chip) * upper) + upper

    def other_chip(turn):
        place = turn + (turn + chips - my_place) // chips
        return place % 2 * (chips - 1) + (1 - 2 * (place % 2)) * (place // 2)

    with jax.named_scope("graphs"):
        total = lax.fori_loop(0, ROUNDS, graph_step, jnp.zeros((evecs, evecs), jnp.float32))
        edge = (total * edge_scale).astype(jnp.bfloat16)
        edges[me] = edge
    landing = inner * (1 + core)
    for turn in range(chips - 1):
        edge_send(me, 1, 2 * other_chip(turn) + 1, landing)

    @pl.when(core == 1)
    def to_first():
        edge_send(me, 1, me - 1, 0)

    @pl.when(core == 0)
    def to_second():
        edge_send(me, 1, me + 1, landing)

    edge_out[0] = edge

    def relay(outer_turns, counts):
        turns = list(range(chips - 1))
        stages = [
            [(2 * other_chip(turn), 2) for turn in turns[:outer_turns]],
            [(2 * other_chip(turn), 1) for turn in turns[outer_turns:]],
            [(2 * other_chip(turn) + 1, 1) for turn in turns[outer_turns:]],
        ]
        for semaphore, (stage, count) in enumerate(zip(stages, counts)):
            with jax.named_scope(f"gather{semaphore}"):
                arrival(edges.at[pl.ds(0, count)], edge_recv_sem.at[semaphore]).wait_recv()
            for owners, width in stage:
                edge_send(owners, width, me - 1, 0)

    half = chips // 2

    @pl.when((core == 1) & (inner == 1))
    def relay_inner():
        relay(half, (chips, half, half - 1))

    @pl.when((core == 1) & (inner == 0))
    def relay_outer():
        relay(half - 1, (chips - 1, half, half))

    @pl.when(core == 0)
    def take_over():
        with jax.named_scope("partner0"):
            arrival(edges.at[pl.ds(0, n - 1)], edge_recv_sem.at[0]).wait_recv()

    with jax.named_scope("pairs"):
        for pair in range(product_out.shape[0]):
            product = jnp.dot(
                edges[pair_ref[0, pair]],
                edges[pair_ref[1, pair]],
                preferred_element_type=jnp.float32,
            )
            product_out[pair] = (product * root_scale).astype(jnp.bfloat16)

    @pl.when(core == 1)
    def sent_by_second():
        all_sent(send_sem.at[1], 3 * chips - 2)

    @pl.when(core == 0)
    def sent_by_first():
        all_sent(send_sem.at[1], chips)


def store_kernel(edge_in, product_in, edge_out, product_out, store_sem):
    edge_copy = pltpu.make_async_copy(edge_in, edge_out, store_sem.at[0])
    product_copy = pltpu.make_async_copy(product_in, product_out, store_sem.at[1])
    edge_copy.start()
    product_copy.start()
    edge_copy.wait()
    product_copy.wait()


def fused_shards(
    n,
    source_slabs,
    sink_slabs,
    perambulators,
    send_pick,
    graph_slot,
    graph_sink,
    graph_count,
    pair_list,
):
    sinks, evecs, _ = sink_slabs.shape
    graphs = graph_slot.shape[1]
    pairs = pair_list.shape[0]
    entries = (graphs + n * sinks) // 2
    vmem = pl.BlockSpec(memory_space=pltpu.VMEM)
    hbm = pl.BlockSpec(memory_space=pltpu.HBM)
    slab = (evecs, evecs)
    held = pl.pallas_call(
        functools.partial(fused_kernel, n, graphs),
        out_shape=(
            pltpu.VMEM((1, *slab), jnp.bfloat16),
            pltpu.VMEM((pairs, *slab), jnp.bfloat16),
        ),
        in_specs=[hbm] * 8,
        out_specs=(vmem, vmem),
        scratch_shapes=[
            pltpu.VMEM((n, *slab), jnp.bfloat16),
            pltpu.VMEM((n, *slab), jnp.bfloat16),
            pltpu.VMEM((n, *slab), jnp.bfloat16),
            pltpu.VMEM((n * sinks + 1, *slab), jnp.bfloat16),
            pltpu.VMEM((2, graphs), jnp.int32),
            pltpu.VMEM((2, graphs), jnp.int32),
            pltpu.VMEM((4, entries), jnp.int32),
            pltpu.SMEM(send_pick.shape, jnp.int32),
            pltpu.SMEM((1,), jnp.int32),
            pltpu.SMEM((2, pairs), jnp.int32),
            pltpu.SMEM((4, entries), jnp.int32),
            pltpu.VMEM(perambulators.shape, jnp.bfloat16),
            pltpu.VMEM(source_slabs.shape, jnp.bfloat16),
            pltpu.VMEM(sink_slabs.shape, jnp.bfloat16),
            pltpu.SemaphoreType.DMA((9,)),
            pltpu.SemaphoreType.DMA((2,)),
            pltpu.SemaphoreType.DMA((n // 2,)),
            pltpu.SemaphoreType.DMA((3,)),
        ],
        compiler_params=pltpu.CompilerParams(
            collective_id=0, has_side_effects=True
        ),
        name="contraction",
    )(
        send_pick,
        graph_slot[0].T,
        graph_sink[0].T,
        graph_count,
        pair_list.T,
        perambulators,
        source_slabs,
        sink_slabs,
    )
    return pl.pallas_call(
        store_kernel,
        out_shape=tuple(jax.ShapeDtypeStruct(part.shape, part.dtype) for part in held),
        in_specs=[vmem, vmem],
        out_specs=(hbm, hbm),
        scratch_shapes=[pltpu.SemaphoreType.DMA((2,))],
        compiler_params=pltpu.CompilerParams(vmem_limit_bytes=1024 * 1024),
        name="store",
    )(*(pltpu.with_memory_space_constraint(part, pltpu.VMEM) for part in held))


def shards(readers, source_slabs, sink_slabs, perambulators, *tables):
    slabs = sink_slabs.shape[0]
    graphs = tables[1].shape[1]
    entries = (graphs + readers * slabs) // 2
    power = readers & (readers - 1) == 0 and readers // 8 == 2
    even = graphs % LANES == 0 and entries % (2 * ROUNDS) == 0 and entries % LANES == 0
    if power and even and readers * slabs <= 2 * graphs and slabs % 4 == 0:
        return fused_shards(readers, source_slabs, sink_slabs, perambulators, *tables)
    return looped_shards(source_slabs, sink_slabs, perambulators, *tables)


def solution(mesh):
    return jax.shard_map(
        functools.partial(shards, mesh.shape["had"]),
        mesh=mesh,
        in_specs=(
            P(("grp", "had"), None, None),
            P(("grp", "had"), None, None),
            P("grp", None, None, None),
            P(("grp", "had"), None),
            P(("grp", "had"), None, None),
            P(("grp", "had"), None, None),
            P(("grp", "had")),
            P(("grp", "had"), None),
        ),
        out_specs=(P(("grp", "had"), None, None), P(("grp", "had"), None, None)),
        check_vma=False,
    )
```

```python
import functools
import math

import jax
import jax.numpy as jnp
from jax import lax
from jax.experimental import pallas as pl
from jax.experimental.pallas import tpu as pltpu
from jax.sharding import PartitionSpec as P


def looped_shards(
    source_slabs,
    sink_slabs,
    perambulators,
    send_pick,
    graph_slot,
    graph_sink,
    graph_count,
    pair_list,
):
    my_index = lax.axis_index("had")
    evecs = source_slabs.shape[1]
    per_device = source_slabs.shape[0]
    root_scale = 1.0 / math.sqrt(evecs)
    edge_scale = 1.0 / math.sqrt(evecs * graph_slot.shape[1])
    timeslice = my_index * per_device // evecs
    local_peram = lax.dynamic_index_in_dim(perambulators, timeslice, 0, keepdims=False)
    first_turn = jnp.einsum(
        "xa,jab->xjb", local_peram[0], source_slabs, preferred_element_type=jnp.float32
    ).astype(jnp.bfloat16)
    pick_row = send_pick[0]
    second_turn = jnp.einsum(
        "xjb,yb->xjy", first_turn, local_peram[1], preferred_element_type=jnp.float32
    ).astype(jnp.bfloat16)
    outgoing = jnp.take(second_turn, pick_row, axis=1)
    received = lax.all_to_all(outgoing, "had", split_axis=1, concat_axis=1, tiled=True)
    graph_rows = graph_slot.shape[1]
    block_width = min(64, graph_rows)
    slot_table = graph_slot[0]
    sink_table = graph_sink[0]
    graph_total = graph_count[0]

    def factor(slots, sinks):
        gathered = jnp.take(received, slots, axis=1)
        resident = jnp.take(sink_slabs, sinks, axis=0)
        product = jnp.einsum("gxb,agb->gxa", resident, gathered, preferred_element_type=jnp.float32)
        return (product * root_scale).astype(jnp.bfloat16)

    def accumulate(block_index, running_sum):
        offset = block_index * block_width
        slots = lax.dynamic_slice_in_dim(slot_table, offset, block_width, 0)
        sinks = lax.dynamic_slice_in_dim(sink_table, offset, block_width, 0)
        is_valid = (offset + jnp.arange(block_width, dtype=jnp.int32) < graph_total).astype(
            jnp.bfloat16
        )
        left_side = factor(slots[:, 0], sinks[:, 0]) * is_valid[:, None, None]
        right_side = factor(slots[:, 1], sinks[:, 1])
        return running_sum + jnp.einsum(
            "gxa,gay->xy", left_side, right_side, preferred_element_type=jnp.float32
        )

    block_count = (graph_total + block_width - 1) // block_width
    summed = lax.fori_loop(0, block_count, accumulate, jnp.zeros((evecs, evecs), jnp.float32))
    edge_local = (summed * edge_scale).astype(jnp.bfloat16)[None]
    left_ids = pair_list[:, 0]
    right_ids = pair_list[:, 1]
    shard_rows = lax.all_gather(edge_local, "had", axis=0, tiled=True)
    row_ids = jnp.arange(shard_rows.shape[0], dtype=jnp.int32)
    left_select = (left_ids[:, None] == row_ids[None, :]).astype(jnp.bfloat16)
    right_select = (right_ids[:, None] == row_ids[None, :]).astype(jnp.bfloat16)
    left_part = jnp.einsum(
        "pn,nxy->pxy", left_select, shard_rows, preferred_element_type=jnp.float32
    )
    right_part = jnp.einsum(
        "pn,nxy->pxy", right_select, shard_rows, preferred_element_type=jnp.float32
    )
    left_edges = left_part.astype(jnp.bfloat16)
    right_edges = right_part.astype(jnp.bfloat16)
    product = jnp.einsum(
        "pxa,pay->pxy", left_edges, right_edges, preferred_element_type=jnp.float32
    )
    pair_products = (product * root_scale).astype(jnp.bfloat16)
    return (edge_local, pair_products)


NT = (((1,), (1,)), ((), ()))
LANES = 128
ROUNDS = 2


def column(values):
    return jnp.concatenate(
        [
            jnp.broadcast_to(values[:, start : start + LANES], (LANES, LANES)).T
            for start in range(0, values.shape[1], LANES)
        ],
        axis=0,
    )


def pair_up(left, right, tables, entries):
    graphs = left.shape[1]
    left_column = column(left)
    turns = lax.broadcasted_iota(jnp.int32, (graphs, LANES), 0)
    lanes = lax.broadcasted_iota(jnp.int32, (graphs, LANES), 1)
    ranks = []
    for start in range(0, graphs, LANES):
        same = left_column == left[:, start : start + LANES]
        ahead = jnp.where(same & (turns < lanes + start), 1, 0)
        ranks.append(jnp.sum(ahead, axis=0, keepdims=True))
    rank = jnp.concatenate(ranks, axis=1)
    opens = jnp.where(column(rank) % 2 == 0, left_column, tables + 1)
    keys = []
    for start in range(0, graphs, LANES):
        below = jnp.where(opens < left[:, start : start + LANES], 2, 0)
        keys.append(jnp.sum(below, axis=0, keepdims=True) + rank[:, start : start + LANES])
    key_column = column(jnp.concatenate(keys, axis=1))
    right_column = column(right) + 1
    shift = 2 * tables
    packed = left_column * shift + right_column
    rows = ([], [], [])
    for start in range(0, entries, LANES):
        here = key_column - 2 * (lanes + start)
        even = jnp.sum(jnp.where(here == 0, packed, 0), axis=0, keepdims=True)
        odd = jnp.sum(jnp.where(here == 1, right_column, 0), axis=0, keepdims=True)
        used = even > 0
        rows[0].append(jnp.where(used, even // shift, tables))
        rows[1].append(jnp.where(used, even % shift - 1, tables))
        rows[2].append(jnp.where(odd > 0, odd - 1, tables))
    return [jnp.concatenate(row, axis=1) for row in rows]


def flip(index, step):
    flipped = index
    bit = 1
    while bit <= step:
        if step & bit:
            flipped = flipped + bit * (1 - 2 * (index // bit % 2))
        bit *= 2
    return flipped


def fused_kernel(
    n,
    graphs,
    pick_in,
    slot_in,
    graph_sink_in,
    count_in,
    pair_in,
    peram_in,
    source_in,
    sink_in,
    edge_out,
    product_out,
    edges,
    outgoing,
    received,
    table,
    slot_ref,
    graph_sink_ref,
    index_ref,
    pick_ref,
    count_ref,
    pair_ref,
    graph_ref,
    peram_ref,
    source_ref,
    sink_ref,
    load_sem,
    send_sem,
    recv_sem,
    edge_recv_sem,
):
    me = lax.axis_index("had")
    per_device, evecs, _ = source_ref.shape
    root_scale = 1.0 / math.sqrt(evecs)
    edge_scale = 1.0 / math.sqrt(evecs * graphs)
    sinks = sink_ref.shape[0]
    entries = graph_ref.shape[1]
    unroll = entries // ROUNDS

    def at(peer):
        return dict(device_id={"had": peer}, device_id_type=pl.DeviceIdType.MESH)

    barrier = pltpu.get_barrier_semaphore()
    for step in range(n - 1, 0, -1):
        pl.semaphore_signal(barrier, inc=1, **at(flip(me, step)))

    loads = {}
    for name, source, target in (
        ("pick", pick_in, pick_ref),
        ("peram", peram_in, peram_ref),
        ("source", source_in, source_ref),
        ("slot", slot_in, slot_ref),
        ("graph_sink", graph_sink_in, graph_sink_ref),
        ("count", count_in, count_ref),
        ("sink", sink_in, sink_ref),
        ("pair", pair_in, pair_ref),
    ):
        loads[name] = pltpu.make_async_copy(source, target, load_sem.at[len(loads)])
        loads[name].start()
    with jax.named_scope("load"):
        for name in ("pick", "peram", "source"):
            loads[name].wait()

    timeslice = me * per_device // evecs
    first = peram_ref[timeslice, 0]
    second = peram_ref[timeslice, 1]
    chips = n // 2
    levels = chips // 2
    chip, core = me // 2, me % 2
    level, row = chip // 2, chip % 2
    upper = chip // levels

    def across(distance, other_row):
        far = (1 - upper) * (chips // 2 - 1 - distance) + upper * distance
        return 2 * far + row + other_row * (1 - 2 * row)

    in_half = level % (levels // 2)
    inner = upper * (1 - in_half) + (1 - upper) * in_half

    def through(distance):
        return [
            (2 * across(distance, other) + side, levels + 2 * other + in_half)
            for side in range(2)
            for other in range(2)
        ]

    near = [flip(chip, step) for step in range(levels)]
    close = []
    for step in range(1, levels):
        close += [(2 * near[step] + 1 - core, step), (2 * near[step] + core, step)]
    peers = through(0) + through(1)[:2] + close + through(1)[2:]
    peers += [(2 * chip + 1 - core, 0), (me, None)]

    def rotate(targets):
        halves = []
        for peer, _ in targets:
            slab = source_ref[pick_ref[0, peer]]
            half = jnp.dot(first, slab, preferred_element_type=jnp.float32)
            halves.append(half.astype(jnp.bfloat16))
        for (peer, _), half in zip(targets, halves):
            turned = lax.dot_general(half, second, NT, preferred_element_type=jnp.float32)
            target = received if peer is me else outgoing
            target[peer] = turned.astype(jnp.bfloat16)

    def send(targets):
        for peer, place in targets:
            if place is not None:
                pltpu.make_async_remote_copy(
                    src_ref=outgoing.at[peer],
                    dst_ref=received.at[me],
                    send_sem=send_sem.at[0],
                    recv_sem=recv_sem.at[place],
                    **at(peer),
                ).start()

    def arrival(buffer, semaphore):
        return pltpu.make_async_remote_copy(
            src_ref=buffer,
            dst_ref=buffer,
            send_sem=send_sem.at[0],
            recv_sem=semaphore,
            **at(2 * chip + 1 - core),
        )

    def all_sent(semaphore, slabs):
        pltpu.make_async_remote_copy(
            src_ref=table.at[pl.ds(0, slabs)],
            dst_ref=table.at[pl.ds(0, slabs)],
            send_sem=semaphore,
            recv_sem=recv_sem.at[0],
            **at(2 * chip + 1 - core),
        ).wait_send()

    group = 4
    for at_group in range(0, n, group):
        targets = peers[at_group : at_group + group]
        with jax.named_scope(f"rotate{at_group}"):
            rotate(targets)
        if at_group == 0:
            with jax.named_scope("meet"):
                pl.semaphore_wait(barrier, n - 1)
        send(targets)

    with jax.named_scope("index"):
        for name in ("slot", "graph_sink", "count"):
            loads[name].wait()
        graph_ids = lax.broadcasted_iota(jnp.int32, slot_ref.shape, 1)
        places = slot_ref[...] * sinks + graph_sink_ref[...]
        left_ids = jnp.where(graph_ids[:1] < count_ref[0], places[:1], n * sinks)
        for place, ids in enumerate(pair_up(left_ids, places[1:], n * sinks, entries)):
            index_ref[place : place + 1] = ids
        index_load = pltpu.make_async_copy(index_ref, graph_ref, load_sem.at[len(loads)])
        index_load.start()
        table[n * sinks] = jnp.zeros((evecs, evecs), jnp.bfloat16)
        rows = 4
        loads["sink"].wait()
        loads["pair"].wait()
        index_load.wait()


    def source(place, other):
        return 2 * ((1 - upper) * (levels // 2) + place) + row + other * (1 - 2 * row)

    from_near = [(near[step], step) for step in range(levels)]
    from_far = [
        (source(place, other), levels + 2 * other + place)
        for other in range(2)
        for place in (upper, 1 - upper)
    ]
    def fill(units, skip=0):
        places = [
            [inner * one + (1 - inner) * two for one, two in zip(*unit)] for unit in units
        ]
        for owner, semaphore in places[skip:]:
            landed = received.at[pl.ds(0, 2)]
            arrival(landed, recv_sem.at[semaphore]).wait_recv()
        for block in range(sinks // rows):
            left = sink_ref[block * rows : (block + 1) * rows].reshape(rows * evecs, evecs)
            for owner, _ in places:
                both = received[pl.ds(2 * owner, 2)].reshape(2 * evecs, evecs)
                product = lax.dot_general(left, both, NT, preferred_element_type=jnp.float32)
                factors = (product * root_scale).astype(jnp.bfloat16)
                for side in range(2):
                    part = factors[:, side * evecs : (side + 1) * evecs].reshape(rows, evecs, evecs)
                    table[pl.ds((2 * owner + side) * sinks + block * rows, rows)] = part

    with jax.named_scope("arrive0"):
        arrival(received.at[0], recv_sem.at[0]).wait_recv()
    order_inner = from_near + from_far
    order_outer = from_near[:2] + from_far + from_near[2:]
    units = list(zip(order_inner, order_outer))
    fill(units[:1], skip=1)
    with jax.named_scope("fill1"):
        fill(units[1:2])
    with jax.named_scope("fill2"):
        fill(units[2:3])
    with jax.named_scope("fill3"):
        fill(units[3:4])
    with jax.named_scope("fill4"):
        fill(units[4:6])
    with jax.named_scope("fill6"):
        fill(units[6:8])
    all_sent(send_sem.at[0], n - 1)

    def graph_step(block, total):
        start = unroll * block
        left = [table[graph_ref[0, start + entry]] for entry in range(unroll)]
        right = [
            jnp.concatenate([table[graph_ref[side, start + entry]] for side in (1, 2)], axis=1)
            for entry in range(unroll)
        ]
        both = jnp.dot(
            jnp.concatenate(left, axis=1),
            jnp.concatenate(right, axis=0),
            preferred_element_type=jnp.float32,
        )
        return total + both[:, :evecs] + both[:, evecs:]

    def edge_send(owners, count, peer, semaphore):
        pltpu.make_async_remote_copy(
            src_ref=edges.at[pl.ds(owners, count)],
            dst_ref=edges.at[pl.ds(owners, count)],
            send_sem=send_sem.at[1],
            recv_sem=edge_recv_sem.at[semaphore],
            **at(peer),
        ).start()

    my_place = 2 * (chip * (1 - upper) + (chips - 1 - chip) * upper) + upper

    def other_chip(turn):
        place = turn + (turn + chips - my_place) // chips
        return place % 2 * (chips - 1) + (1 - 2 * (place % 2)) * (place // 2)

    with jax.named_scope("graphs"):
        total = lax.fori_loop(0, ROUNDS, graph_step, jnp.zeros((evecs, evecs), jnp.float32))
        edge = (total * edge_scale).astype(jnp.bfloat16)
        edges[me] = edge
    landing = inner * (1 + core)
    far_outer = across(0, 0)
    ring = across(0, 1)

    @pl.when(inner == 1)
    def spread_inner():
        for turn in range(chips - 1):
            edge_send(me, 1, 2 * other_chip(turn) + 1, landing)

    @pl.when(inner == 0)
    def spread_outer():
        edge_send(me, 1, 2 * far_outer + 1, 0)
        edge_send(me, 1, 2 * ring + 1, 0)
        edge_send(me, 1, 2 * across(1, 0) + 1, 3)
        for target in near[1:]:
            edge_send(me, 1, 2 * target + 1, 0)

    @pl.when(core == 1)
    def to_first():
        edge_send(me, 1, me - 1, 0)

    @pl.when(core == 0)
    def to_second():
        edge_send(me, 1, me + 1, landing)

    edge_out[0] = edge

    inners = {1: [near[1], across(1, 0), across(1, 1)], 0: near[2:] + [across(1, 0), across(1, 1)]}
    outers = {1: near[2:] + [ring], 0: [near[1], far_outer, ring]}
    own = {1: (0, 1), 0: (1, 0)}
    relayed = {}

    def relay(kind):
        stages = [
            (3, 2, [(far_outer, 0, 2)]),
            (0, 2 * len(outers[kind]) + own[kind][0], [(chip_of, 0, 2) for chip_of in outers[kind]]),
            (1, len(inners[kind]) + own[kind][1], [(chip_of, 0, 1) for chip_of in inners[kind]]),
            (2, len(inners[kind]), [(chip_of, 1, 1) for chip_of in inners[kind]]),
        ]
        if kind == 0:
            stages = stages[1:]
        relayed[kind] = 2 * kind + sum(width for _, _, stage in stages for _, _, width in stage)
        for semaphore, count, stage in stages:
            with jax.named_scope(f"gather{semaphore}"):
                arrival(edges.at[pl.ds(0, count)], edge_recv_sem.at[semaphore]).wait_recv()
            for chip_of, side, width in stage:
                if semaphore == 3:
                    edge_send(2 * chip_of, width, 2 * near[1] + 1, 0)
                edge_send(2 * chip_of + side, width, me - 1, 0)

    for kind in range(2):
        pl.when((core == 1) & (inner == kind))(functools.partial(relay, kind))

    @pl.when(core == 0)
    def take_over():
        with jax.named_scope("partner0"):
            arrival(edges.at[pl.ds(0, n - 1)], edge_recv_sem.at[0]).wait_recv()

    with jax.named_scope("pairs"):
        for pair in range(product_out.shape[0]):
            product = jnp.dot(
                edges[pair_ref[0, pair]],
                edges[pair_ref[1, pair]],
                preferred_element_type=jnp.float32,
            )
            product_out[pair] = (product * root_scale).astype(jnp.bfloat16)

    for kind, spread in ((0, levels + 3), (1, chips)):
        for side in range(2):
            slabs = spread + side * relayed[kind]
            pl.when((core == side) & (inner == kind))(
                functools.partial(all_sent, send_sem.at[1], slabs)
            )


def store_kernel(edge_in, product_in, edge_out, product_out, store_sem):
    edge_copy = pltpu.make_async_copy(edge_in, edge_out, store_sem.at[0])
    product_copy = pltpu.make_async_copy(product_in, product_out, store_sem.at[1])
    edge_copy.start()
    product_copy.start()
    edge_copy.wait()
    product_copy.wait()


def fused_shards(
    n,
    source_slabs,
    sink_slabs,
    perambulators,
    send_pick,
    graph_slot,
    graph_sink,
    graph_count,
    pair_list,
):
    sinks, evecs, _ = sink_slabs.shape
    graphs = graph_slot.shape[1]
    pairs = pair_list.shape[0]
    entries = (graphs + n * sinks) // 2
    vmem = pl.BlockSpec(memory_space=pltpu.VMEM)
    hbm = pl.BlockSpec(memory_space=pltpu.HBM)
    slab = (evecs, evecs)
    held = pl.pallas_call(
        functools.partial(fused_kernel, n, graphs),
        out_shape=(
            pltpu.VMEM((1, *slab), jnp.bfloat16),
            pltpu.VMEM((pairs, *slab), jnp.bfloat16),
        ),
        in_specs=[hbm] * 8,
        out_specs=(vmem, vmem),
        scratch_shapes=[
            pltpu.VMEM((n, *slab), jnp.bfloat16),
            pltpu.VMEM((n, *slab), jnp.bfloat16),
            pltpu.VMEM((n, *slab), jnp.bfloat16),
            pltpu.VMEM((n * sinks + 1, *slab), jnp.bfloat16),
            pltpu.VMEM((2, graphs), jnp.int32),
            pltpu.VMEM((2, graphs), jnp.int32),
            pltpu.VMEM((4, entries), jnp.int32),
            pltpu.SMEM(send_pick.shape, jnp.int32),
            pltpu.SMEM((1,), jnp.int32),
            pltpu.SMEM((2, pairs), jnp.int32),
            pltpu.SMEM((4, entries), jnp.int32),
            pltpu.VMEM(perambulators.shape, jnp.bfloat16),
            pltpu.VMEM(source_slabs.shape, jnp.bfloat16),
            pltpu.VMEM(sink_slabs.shape, jnp.bfloat16),
            pltpu.SemaphoreType.DMA((9,)),
            pltpu.SemaphoreType.DMA((2,)),
            pltpu.SemaphoreType.DMA((n // 2,)),
            pltpu.SemaphoreType.DMA((4,)),
        ],
        compiler_params=pltpu.CompilerParams(
            collective_id=0, has_side_effects=True
        ),
        name="contraction",
    )(
        send_pick,
        graph_slot[0].T,
        graph_sink[0].T,
        graph_count,
        pair_list.T,
        perambulators,
        source_slabs,
        sink_slabs,
    )
    return pl.pallas_call(
        store_kernel,
        out_shape=tuple(jax.ShapeDtypeStruct(part.shape, part.dtype) for part in held),
        in_specs=[vmem, vmem],
        out_specs=(hbm, hbm),
        scratch_shapes=[pltpu.SemaphoreType.DMA((2,))],
        compiler_params=pltpu.CompilerParams(vmem_limit_bytes=1024 * 1024),
        name="store",
    )(*(pltpu.with_memory_space_constraint(part, pltpu.VMEM) for part in held))


def shards(readers, source_slabs, sink_slabs, perambulators, *tables):
    slabs = sink_slabs.shape[0]
    graphs = tables[1].shape[1]
    entries = (graphs + readers * slabs) // 2
    power = readers & (readers - 1) == 0 and readers // 8 == 2
    even = graphs % LANES == 0 and entries % (2 * ROUNDS) == 0 and entries % LANES == 0
    if power and even and readers * slabs <= 2 * graphs and slabs % 4 == 0:
        return fused_shards(readers, source_slabs, sink_slabs, perambulators, *tables)
    return looped_shards(source_slabs, sink_slabs, perambulators, *tables)


def solution(mesh):
    return jax.shard_map(
        functools.partial(shards, mesh.shape["had"]),
        mesh=mesh,
        in_specs=(
            P(("grp", "had"), None, None),
            P(("grp", "had"), None, None),
            P("grp", None, None, None),
            P(("grp", "had"), None),
            P(("grp", "had"), None, None),
            P(("grp", "had"), None, None),
            P(("grp", "had")),
            P(("grp", "had"), None),
        ),
        out_specs=(P(("grp", "had"), None, None), P(("grp", "had"), None, None)),
        check_vma=False,
    )
```

```python
import functools
import math

import jax
import jax.numpy as jnp
from jax import lax
from jax.experimental import pallas as pl
from jax.experimental.pallas import tpu as pltpu
from jax.sharding import PartitionSpec as P


def looped_shards(
    source_slabs,
    sink_slabs,
    perambulators,
    send_pick,
    graph_slot,
    graph_sink,
    graph_count,
    pair_list,
):
    my_index = lax.axis_index("had")
    evecs = source_slabs.shape[1]
    per_device = source_slabs.shape[0]
    root_scale = 1.0 / math.sqrt(evecs)
    edge_scale = 1.0 / math.sqrt(evecs * graph_slot.shape[1])
    timeslice = my_index * per_device // evecs
    local_peram = lax.dynamic_index_in_dim(perambulators, timeslice, 0, keepdims=False)
    first_turn = jnp.einsum(
        "xa,jab->xjb", local_peram[0], source_slabs, preferred_element_type=jnp.float32
    ).astype(jnp.bfloat16)
    pick_row = send_pick[0]
    second_turn = jnp.einsum(
        "xjb,yb->xjy", first_turn, local_peram[1], preferred_element_type=jnp.float32
    ).astype(jnp.bfloat16)
    outgoing = jnp.take(second_turn, pick_row, axis=1)
    received = lax.all_to_all(outgoing, "had", split_axis=1, concat_axis=1, tiled=True)
    graph_rows = graph_slot.shape[1]
    block_width = min(64, graph_rows)
    slot_table = graph_slot[0]
    sink_table = graph_sink[0]
    graph_total = graph_count[0]

    def factor(slots, sinks):
        gathered = jnp.take(received, slots, axis=1)
        resident = jnp.take(sink_slabs, sinks, axis=0)
        product = jnp.einsum("gxb,agb->gxa", resident, gathered, preferred_element_type=jnp.float32)
        return (product * root_scale).astype(jnp.bfloat16)

    def accumulate(block_index, running_sum):
        offset = block_index * block_width
        slots = lax.dynamic_slice_in_dim(slot_table, offset, block_width, 0)
        sinks = lax.dynamic_slice_in_dim(sink_table, offset, block_width, 0)
        is_valid = (offset + jnp.arange(block_width, dtype=jnp.int32) < graph_total).astype(
            jnp.bfloat16
        )
        left_side = factor(slots[:, 0], sinks[:, 0]) * is_valid[:, None, None]
        right_side = factor(slots[:, 1], sinks[:, 1])
        return running_sum + jnp.einsum(
            "gxa,gay->xy", left_side, right_side, preferred_element_type=jnp.float32
        )

    block_count = (graph_total + block_width - 1) // block_width
    summed = lax.fori_loop(0, block_count, accumulate, jnp.zeros((evecs, evecs), jnp.float32))
    edge_local = (summed * edge_scale).astype(jnp.bfloat16)[None]
    left_ids = pair_list[:, 0]
    right_ids = pair_list[:, 1]
    shard_rows = lax.all_gather(edge_local, "had", axis=0, tiled=True)
    row_ids = jnp.arange(shard_rows.shape[0], dtype=jnp.int32)
    left_select = (left_ids[:, None] == row_ids[None, :]).astype(jnp.bfloat16)
    right_select = (right_ids[:, None] == row_ids[None, :]).astype(jnp.bfloat16)
    left_part = jnp.einsum(
        "pn,nxy->pxy", left_select, shard_rows, preferred_element_type=jnp.float32
    )
    right_part = jnp.einsum(
        "pn,nxy->pxy", right_select, shard_rows, preferred_element_type=jnp.float32
    )
    left_edges = left_part.astype(jnp.bfloat16)
    right_edges = right_part.astype(jnp.bfloat16)
    product = jnp.einsum(
        "pxa,pay->pxy", left_edges, right_edges, preferred_element_type=jnp.float32
    )
    pair_products = (product * root_scale).astype(jnp.bfloat16)
    return (edge_local, pair_products)


NT = (((1,), (1,)), ((), ()))
LANES = 128
ROUNDS = 2


def column(values):
    return jnp.concatenate(
        [
            jnp.broadcast_to(values[:, start : start + LANES], (LANES, LANES)).T
            for start in range(0, values.shape[1], LANES)
        ],
        axis=0,
    )


def pair_up(left, right, tables, entries):
    graphs = left.shape[1]
    left_column = column(left)
    turns = lax.broadcasted_iota(jnp.int32, (graphs, LANES), 0)
    lanes = lax.broadcasted_iota(jnp.int32, (graphs, LANES), 1)
    ranks = []
    for start in range(0, graphs, LANES):
        same = left_column == left[:, start : start + LANES]
        ahead = jnp.where(same & (turns < lanes + start), 1, 0)
        ranks.append(jnp.sum(ahead, axis=0, keepdims=True))
    rank = jnp.concatenate(ranks, axis=1)
    opens = jnp.where(column(rank) % 2 == 0, left_column, tables + 1)
    keys = []
    for start in range(0, graphs, LANES):
        below = jnp.where(opens < left[:, start : start + LANES], 2, 0)
        keys.append(jnp.sum(below, axis=0, keepdims=True) + rank[:, start : start + LANES])
    key_column = column(jnp.concatenate(keys, axis=1))
    right_column = column(right) + 1
    shift = 2 * tables
    packed = left_column * shift + right_column
    rows = ([], [], [])
    for start in range(0, entries, LANES):
        here = key_column - 2 * (lanes + start)
        even = jnp.sum(jnp.where(here == 0, packed, 0), axis=0, keepdims=True)
        odd = jnp.sum(jnp.where(here == 1, right_column, 0), axis=0, keepdims=True)
        used = even > 0
        rows[0].append(jnp.where(used, even // shift, tables))
        rows[1].append(jnp.where(used, even % shift - 1, tables))
        rows[2].append(jnp.where(odd > 0, odd - 1, tables))
    return [jnp.concatenate(row, axis=1) for row in rows]


def flip(index, step):
    flipped = index
    bit = 1
    while bit <= step:
        if step & bit:
            flipped = flipped + bit * (1 - 2 * (index // bit % 2))
        bit *= 2
    return flipped


def fused_kernel(
    n,
    graphs,
    pick_in,
    slot_in,
    graph_sink_in,
    count_in,
    pair_in,
    peram_in,
    source_in,
    sink_in,
    edge_out,
    product_out,
    edges,
    outgoing,
    received,
    table,
    slot_ref,
    graph_sink_ref,
    index_ref,
    pick_ref,
    count_ref,
    pair_ref,
    graph_ref,
    peram_ref,
    source_ref,
    sink_ref,
    load_sem,
    send_sem,
    recv_sem,
    edge_recv_sem,
):
    me = lax.axis_index("had")
    per_device, evecs, _ = source_ref.shape
    root_scale = 1.0 / math.sqrt(evecs)
    edge_scale = 1.0 / math.sqrt(evecs * graphs)
    sinks = sink_ref.shape[0]
    entries = graph_ref.shape[1]
    unroll = entries // ROUNDS

    def at(peer):
        return dict(device_id={"had": peer}, device_id_type=pl.DeviceIdType.MESH)

    barrier = pltpu.get_barrier_semaphore()
    for step in range(n - 1, 0, -1):
        pl.semaphore_signal(barrier, inc=1, **at(flip(me, step)))

    loads = {}
    for name, source, target in (
        ("pick", pick_in, pick_ref),
        ("peram", peram_in, peram_ref),
        ("source", source_in, source_ref),
        ("slot", slot_in, slot_ref),
        ("graph_sink", graph_sink_in, graph_sink_ref),
        ("count", count_in, count_ref),
        ("sink", sink_in, sink_ref),
        ("pair", pair_in, pair_ref),
    ):
        loads[name] = pltpu.make_async_copy(source, target, load_sem.at[len(loads)])
        loads[name].start()
    with jax.named_scope("load"):
        for name in ("pick", "peram", "source"):
            loads[name].wait()

    timeslice = me * per_device // evecs
    first = peram_ref[timeslice, 0]
    second = peram_ref[timeslice, 1]
    chips = n // 2
    levels = chips // 2
    chip, core = me // 2, me % 2
    level, row = chip // 2, chip % 2
    upper = chip // levels

    def across(distance, other_row):
        far = (1 - upper) * (chips // 2 - 1 - distance) + upper * distance
        return 2 * far + row + other_row * (1 - 2 * row)

    in_half = level % (levels // 2)
    inner = upper * (1 - in_half) + (1 - upper) * in_half

    def through(distance):
        return [
            (2 * across(distance, other) + side, levels + 2 * other + in_half)
            for side in range(2)
            for other in range(2)
        ]

    near = [flip(chip, step) for step in range(levels)]
    close = []
    for step in range(1, levels):
        close += [(2 * near[step] + 1 - core, step), (2 * near[step] + core, step)]
    first_order = through(0) + through(1)[:2] + close + through(1)[2:]
    second_order = close + through(0) + through(1)
    peers = [
        tuple(core * two + (1 - core) * one for one, two in zip(*both))
        for both in zip(first_order, second_order)
    ]
    peers += [(2 * chip + 1 - core, 0), (me, None)]

    def rotate(targets):
        halves = []
        for peer, _ in targets:
            slab = source_ref[pick_ref[0, peer]]
            half = jnp.dot(first, slab, preferred_element_type=jnp.float32)
            halves.append(half.astype(jnp.bfloat16))
        for (peer, _), half in zip(targets, halves):
            turned = lax.dot_general(half, second, NT, preferred_element_type=jnp.float32)
            target = received if peer is me else outgoing
            target[peer] = turned.astype(jnp.bfloat16)

    def send(targets):
        for peer, place in targets:
            if place is not None:
                pltpu.make_async_remote_copy(
                    src_ref=outgoing.at[peer],
                    dst_ref=received.at[me],
                    send_sem=send_sem.at[0],
                    recv_sem=recv_sem.at[place],
                    **at(peer),
                ).start()

    def arrival(buffer, semaphore):
        return pltpu.make_async_remote_copy(
            src_ref=buffer,
            dst_ref=buffer,
            send_sem=send_sem.at[0],
            recv_sem=semaphore,
            **at(2 * chip + 1 - core),
        )

    def all_sent(semaphore, slabs):
        pltpu.make_async_remote_copy(
            src_ref=table.at[pl.ds(0, slabs)],
            dst_ref=table.at[pl.ds(0, slabs)],
            send_sem=semaphore,
            recv_sem=recv_sem.at[0],
            **at(2 * chip + 1 - core),
        ).wait_send()

    group = 4
    for at_group in range(0, n, group):
        targets = peers[at_group : at_group + group]
        with jax.named_scope(f"rotate{at_group}"):
            rotate(targets)
        if at_group == 0:
            with jax.named_scope("meet"):
                pl.semaphore_wait(barrier, n - 1)
        send(targets)

    with jax.named_scope("index"):
        for name in ("slot", "graph_sink", "count"):
            loads[name].wait()
        graph_ids = lax.broadcasted_iota(jnp.int32, slot_ref.shape, 1)
        places = slot_ref[...] * sinks + graph_sink_ref[...]
        left_ids = jnp.where(graph_ids[:1] < count_ref[0], places[:1], n * sinks)
        for place, ids in enumerate(pair_up(left_ids, places[1:], n * sinks, entries)):
            index_ref[place : place + 1] = ids
        index_load = pltpu.make_async_copy(index_ref, graph_ref, load_sem.at[len(loads)])
        index_load.start()
        table[n * sinks] = jnp.zeros((evecs, evecs), jnp.bfloat16)
        rows = 4
        loads["sink"].wait()
        loads["pair"].wait()
        index_load.wait()


    def source(place, other):
        return 2 * ((1 - upper) * (levels // 2) + place) + row + other * (1 - 2 * row)

    from_near = [(near[step], step) for step in range(levels)]
    from_far = [
        (source(place, other), levels + 2 * other + place)
        for other in range(2)
        for place in (upper, 1 - upper)
    ]
    def fill(units, skip=0):
        places = [
            [inner * one + (1 - inner) * two for one, two in zip(*unit)] for unit in units
        ]
        for owner, semaphore in places[skip:]:
            landed = received.at[pl.ds(0, 2)]
            arrival(landed, recv_sem.at[semaphore]).wait_recv()
        for block in range(sinks // rows):
            left = sink_ref[block * rows : (block + 1) * rows].reshape(rows * evecs, evecs)
            for owner, _ in places:
                both = received[pl.ds(2 * owner, 2)].reshape(2 * evecs, evecs)
                product = lax.dot_general(left, both, NT, preferred_element_type=jnp.float32)
                factors = (product * root_scale).astype(jnp.bfloat16)
                for side in range(2):
                    part = factors[:, side * evecs : (side + 1) * evecs].reshape(rows, evecs, evecs)
                    table[pl.ds((2 * owner + side) * sinks + block * rows, rows)] = part

    with jax.named_scope("arrive0"):
        arrival(received.at[0], recv_sem.at[0]).wait_recv()
    order_inner = from_near + from_far
    order_outer = from_near[:2] + from_far + from_near[2:]
    units = list(zip(order_inner, order_outer))
    fill(units[:1], skip=1)
    with jax.named_scope("fill1"):
        fill(units[1:2])
    with jax.named_scope("fill2"):
        fill(units[2:3])
    with jax.named_scope("fill3"):
        fill(units[3:4])
    with jax.named_scope("fill4"):
        fill(units[4:6])
    with jax.named_scope("fill6"):
        fill(units[6:8])
    all_sent(send_sem.at[0], n - 1)

    def graph_step(block, total):
        start = unroll * block
        left = [table[graph_ref[0, start + entry]] for entry in range(unroll)]
        right = [
            jnp.concatenate([table[graph_ref[side, start + entry]] for side in (1, 2)], axis=1)
            for entry in range(unroll)
        ]
        both = jnp.dot(
            jnp.concatenate(left, axis=1),
            jnp.concatenate(right, axis=0),
            preferred_element_type=jnp.float32,
        )
        return total + both[:, :evecs] + both[:, evecs:]

    def edge_send(owners, count, peer, semaphore):
        pltpu.make_async_remote_copy(
            src_ref=edges.at[pl.ds(owners, count)],
            dst_ref=edges.at[pl.ds(owners, count)],
            send_sem=send_sem.at[1],
            recv_sem=edge_recv_sem.at[semaphore],
            **at(peer),
        ).start()

    my_place = 2 * (chip * (1 - upper) + (chips - 1 - chip) * upper) + upper

    def other_chip(turn):
        place = turn + (turn + chips - my_place) // chips
        return place % 2 * (chips - 1) + (1 - 2 * (place % 2)) * (place // 2)

    with jax.named_scope("graphs"):
        total = lax.fori_loop(0, ROUNDS, graph_step, jnp.zeros((evecs, evecs), jnp.float32))
        edge = (total * edge_scale).astype(jnp.bfloat16)
        edges[me] = edge
    landing = inner * (1 + core)
    far_outer = across(0, 0)
    ring = across(0, 1)

    @pl.when(inner == 1)
    def spread_inner():
        for turn in range(chips - 1):
            edge_send(me, 1, 2 * other_chip(turn) + 1, landing)

    @pl.when(inner == 0)
    def spread_outer():
        edge_send(me, 1, 2 * far_outer + 1, 0)
        edge_send(me, 1, 2 * ring + 1, 0)
        edge_send(me, 1, 2 * across(1, 0) + 1, 3)
        for target in near[1:]:
            edge_send(me, 1, 2 * target + 1, 0)

    @pl.when(core == 1)
    def to_first():
        edge_send(me, 1, me - 1, 0)

    @pl.when(core == 0)
    def to_second():
        edge_send(me, 1, me + 1, landing)

    edge_out[0] = edge

    inners = {1: [near[1], across(1, 0), across(1, 1)], 0: near[2:] + [across(1, 0), across(1, 1)]}
    outers = {1: near[2:] + [ring], 0: [near[1], far_outer, ring]}
    own = {1: (0, 1), 0: (1, 0)}
    relayed = {}

    def relay(kind):
        stages = [
            (3, 2, [(far_outer, 0, 2)]),
            (0, 2 * len(outers[kind]) + own[kind][0], [(chip_of, 0, 2) for chip_of in outers[kind]]),
            (1, len(inners[kind]) + own[kind][1], [(chip_of, 0, 1) for chip_of in inners[kind]]),
            (2, len(inners[kind]), [(chip_of, 1, 1) for chip_of in inners[kind]]),
        ]
        if kind == 0:
            stages = stages[1:]
        relayed[kind] = 2 * kind + sum(width for _, _, stage in stages for _, _, width in stage)
        for semaphore, count, stage in stages:
            with jax.named_scope(f"gather{semaphore}"):
                arrival(edges.at[pl.ds(0, count)], edge_recv_sem.at[semaphore]).wait_recv()
            for chip_of, side, width in stage:
                if semaphore == 3:
                    edge_send(2 * chip_of, width, 2 * near[1] + 1, 0)
                edge_send(2 * chip_of + side, width, me - 1, 0)

    for kind in range(2):
        pl.when((core == 1) & (inner == kind))(functools.partial(relay, kind))

    @pl.when(core == 0)
    def take_over():
        with jax.named_scope("partner0"):
            arrival(edges.at[pl.ds(0, n - 1)], edge_recv_sem.at[0]).wait_recv()

    with jax.named_scope("pairs"):
        for pair in range(product_out.shape[0]):
            product = jnp.dot(
                edges[pair_ref[0, pair]],
                edges[pair_ref[1, pair]],
                preferred_element_type=jnp.float32,
            )
            product_out[pair] = (product * root_scale).astype(jnp.bfloat16)

    for kind, spread in ((0, levels + 3), (1, chips)):
        for side in range(2):
            slabs = spread + side * relayed[kind]
            pl.when((core == side) & (inner == kind))(
                functools.partial(all_sent, send_sem.at[1], slabs)
            )


def store_kernel(edge_in, product_in, edge_out, product_out, store_sem):
    edge_copy = pltpu.make_async_copy(edge_in, edge_out, store_sem.at[0])
    product_copy = pltpu.make_async_copy(product_in, product_out, store_sem.at[1])
    edge_copy.start()
    product_copy.start()
    edge_copy.wait()
    product_copy.wait()


def fused_shards(
    n,
    source_slabs,
    sink_slabs,
    perambulators,
    send_pick,
    graph_slot,
    graph_sink,
    graph_count,
    pair_list,
):
    sinks, evecs, _ = sink_slabs.shape
    graphs = graph_slot.shape[1]
    pairs = pair_list.shape[0]
    entries = (graphs + n * sinks) // 2
    vmem = pl.BlockSpec(memory_space=pltpu.VMEM)
    hbm = pl.BlockSpec(memory_space=pltpu.HBM)
    slab = (evecs, evecs)
    held = pl.pallas_call(
        functools.partial(fused_kernel, n, graphs),
        out_shape=(
            pltpu.VMEM((1, *slab), jnp.bfloat16),
            pltpu.VMEM((pairs, *slab), jnp.bfloat16),
        ),
        in_specs=[hbm] * 8,
        out_specs=(vmem, vmem),
        scratch_shapes=[
            pltpu.VMEM((n, *slab), jnp.bfloat16),
            pltpu.VMEM((n, *slab), jnp.bfloat16),
            pltpu.VMEM((n, *slab), jnp.bfloat16),
            pltpu.VMEM((n * sinks + 1, *slab), jnp.bfloat16),
            pltpu.VMEM((2, graphs), jnp.int32),
            pltpu.VMEM((2, graphs), jnp.int32),
            pltpu.VMEM((4, entries), jnp.int32),
            pltpu.SMEM(send_pick.shape, jnp.int32),
            pltpu.SMEM((1,), jnp.int32),
            pltpu.SMEM((2, pairs), jnp.int32),
            pltpu.SMEM((4, entries), jnp.int32),
            pltpu.VMEM(perambulators.shape, jnp.bfloat16),
            pltpu.VMEM(source_slabs.shape, jnp.bfloat16),
            pltpu.VMEM(sink_slabs.shape, jnp.bfloat16),
            pltpu.SemaphoreType.DMA((9,)),
            pltpu.SemaphoreType.DMA((2,)),
            pltpu.SemaphoreType.DMA((n // 2,)),
            pltpu.SemaphoreType.DMA((4,)),
        ],
        compiler_params=pltpu.CompilerParams(
            collective_id=0, has_side_effects=True
        ),
        name="contraction",
    )(
        send_pick,
        graph_slot[0].T,
        graph_sink[0].T,
        graph_count,
        pair_list.T,
        perambulators,
        source_slabs,
        sink_slabs,
    )
    return pl.pallas_call(
        store_kernel,
        out_shape=tuple(jax.ShapeDtypeStruct(part.shape, part.dtype) for part in held),
        in_specs=[vmem, vmem],
        out_specs=(hbm, hbm),
        scratch_shapes=[pltpu.SemaphoreType.DMA((2,))],
        compiler_params=pltpu.CompilerParams(vmem_limit_bytes=1024 * 1024),
        name="store",
    )(*(pltpu.with_memory_space_constraint(part, pltpu.VMEM) for part in held))


def shards(readers, source_slabs, sink_slabs, perambulators, *tables):
    slabs = sink_slabs.shape[0]
    graphs = tables[1].shape[1]
    entries = (graphs + readers * slabs) // 2
    power = readers & (readers - 1) == 0 and readers // 8 == 2
    even = graphs % LANES == 0 and entries % (2 * ROUNDS) == 0 and entries % LANES == 0
    if power and even and readers * slabs <= 2 * graphs and slabs % 4 == 0:
        return fused_shards(readers, source_slabs, sink_slabs, perambulators, *tables)
    return looped_shards(source_slabs, sink_slabs, perambulators, *tables)


def solution(mesh):
    return jax.shard_map(
        functools.partial(shards, mesh.shape["had"]),
        mesh=mesh,
        in_specs=(
            P(("grp", "had"), None, None),
            P(("grp", "had"), None, None),
            P("grp", None, None, None),
            P(("grp", "had"), None),
            P(("grp", "had"), None, None),
            P(("grp", "had"), None, None),
            P(("grp", "had")),
            P(("grp", "had"), None),
        ),
        out_specs=(P(("grp", "had"), None, None), P(("grp", "had"), None, None)),
        check_vma=False,
    )
```

```python
import functools
import math

import jax
import jax.numpy as jnp
from jax import lax
from jax.experimental import pallas as pl
from jax.experimental.pallas import tpu as pltpu
from jax.sharding import PartitionSpec as P


def looped_shards(
    source_slabs,
    sink_slabs,
    perambulators,
    send_pick,
    graph_slot,
    graph_sink,
    graph_count,
    pair_list,
):
    my_index = lax.axis_index("had")
    evecs = source_slabs.shape[1]
    per_device = source_slabs.shape[0]
    root_scale = 1.0 / math.sqrt(evecs)
    edge_scale = 1.0 / math.sqrt(evecs * graph_slot.shape[1])
    timeslice = my_index * per_device // evecs
    local_peram = lax.dynamic_index_in_dim(perambulators, timeslice, 0, keepdims=False)
    first_turn = jnp.einsum(
        "xa,jab->xjb", local_peram[0], source_slabs, preferred_element_type=jnp.float32
    ).astype(jnp.bfloat16)
    pick_row = send_pick[0]
    second_turn = jnp.einsum(
        "xjb,yb->xjy", first_turn, local_peram[1], preferred_element_type=jnp.float32
    ).astype(jnp.bfloat16)
    outgoing = jnp.take(second_turn, pick_row, axis=1)
    received = lax.all_to_all(outgoing, "had", split_axis=1, concat_axis=1, tiled=True)
    graph_rows = graph_slot.shape[1]
    block_width = min(64, graph_rows)
    slot_table = graph_slot[0]
    sink_table = graph_sink[0]
    graph_total = graph_count[0]

    def factor(slots, sinks):
        gathered = jnp.take(received, slots, axis=1)
        resident = jnp.take(sink_slabs, sinks, axis=0)
        product = jnp.einsum("gxb,agb->gxa", resident, gathered, preferred_element_type=jnp.float32)
        return (product * root_scale).astype(jnp.bfloat16)

    def accumulate(block_index, running_sum):
        offset = block_index * block_width
        slots = lax.dynamic_slice_in_dim(slot_table, offset, block_width, 0)
        sinks = lax.dynamic_slice_in_dim(sink_table, offset, block_width, 0)
        is_valid = (offset + jnp.arange(block_width, dtype=jnp.int32) < graph_total).astype(
            jnp.bfloat16
        )
        left_side = factor(slots[:, 0], sinks[:, 0]) * is_valid[:, None, None]
        right_side = factor(slots[:, 1], sinks[:, 1])
        return running_sum + jnp.einsum(
            "gxa,gay->xy", left_side, right_side, preferred_element_type=jnp.float32
        )

    block_count = (graph_total + block_width - 1) // block_width
    summed = lax.fori_loop(0, block_count, accumulate, jnp.zeros((evecs, evecs), jnp.float32))
    edge_local = (summed * edge_scale).astype(jnp.bfloat16)[None]
    left_ids = pair_list[:, 0]
    right_ids = pair_list[:, 1]
    shard_rows = lax.all_gather(edge_local, "had", axis=0, tiled=True)
    row_ids = jnp.arange(shard_rows.shape[0], dtype=jnp.int32)
    left_select = (left_ids[:, None] == row_ids[None, :]).astype(jnp.bfloat16)
    right_select = (right_ids[:, None] == row_ids[None, :]).astype(jnp.bfloat16)
    left_part = jnp.einsum(
        "pn,nxy->pxy", left_select, shard_rows, preferred_element_type=jnp.float32
    )
    right_part = jnp.einsum(
        "pn,nxy->pxy", right_select, shard_rows, preferred_element_type=jnp.float32
    )
    left_edges = left_part.astype(jnp.bfloat16)
    right_edges = right_part.astype(jnp.bfloat16)
    product = jnp.einsum(
        "pxa,pay->pxy", left_edges, right_edges, preferred_element_type=jnp.float32
    )
    pair_products = (product * root_scale).astype(jnp.bfloat16)
    return (edge_local, pair_products)


NT = (((1,), (1,)), ((), ()))
LANES = 128
ROUNDS = 2


def column(values):
    return jnp.concatenate(
        [
            jnp.broadcast_to(values[:, start : start + LANES], (LANES, LANES)).T
            for start in range(0, values.shape[1], LANES)
        ],
        axis=0,
    )


def pair_up(left, right, tables, entries):
    graphs = left.shape[1]
    left_column = column(left)
    turns = lax.broadcasted_iota(jnp.int32, (graphs, LANES), 0)
    lanes = lax.broadcasted_iota(jnp.int32, (graphs, LANES), 1)
    ranks = []
    for start in range(0, graphs, LANES):
        same = left_column == left[:, start : start + LANES]
        ahead = jnp.where(same & (turns < lanes + start), 1, 0)
        ranks.append(jnp.sum(ahead, axis=0, keepdims=True))
    rank = jnp.concatenate(ranks, axis=1)
    opens = jnp.where(column(rank) % 2 == 0, left_column, tables + 1)
    keys = []
    for start in range(0, graphs, LANES):
        below = jnp.where(opens < left[:, start : start + LANES], 2, 0)
        keys.append(jnp.sum(below, axis=0, keepdims=True) + rank[:, start : start + LANES])
    key_column = column(jnp.concatenate(keys, axis=1))
    right_column = column(right) + 1
    shift = 2 * tables
    packed = left_column * shift + right_column
    rows = ([], [], [])
    for start in range(0, entries, LANES):
        here = key_column - 2 * (lanes + start)
        even = jnp.sum(jnp.where(here == 0, packed, 0), axis=0, keepdims=True)
        odd = jnp.sum(jnp.where(here == 1, right_column, 0), axis=0, keepdims=True)
        used = even > 0
        rows[0].append(jnp.where(used, even // shift, tables))
        rows[1].append(jnp.where(used, even % shift - 1, tables))
        rows[2].append(jnp.where(odd > 0, odd - 1, tables))
    return [jnp.concatenate(row, axis=1) for row in rows]


def flip(index, step):
    flipped = index
    bit = 1
    while bit <= step:
        if step & bit:
            flipped = flipped + bit * (1 - 2 * (index // bit % 2))
        bit *= 2
    return flipped


def fused_kernel(
    n,
    graphs,
    pick_in,
    slot_in,
    graph_sink_in,
    count_in,
    pair_in,
    peram_in,
    source_in,
    sink_in,
    edge_out,
    product_out,
    edges,
    outgoing,
    received,
    table,
    slot_ref,
    graph_sink_ref,
    index_ref,
    pick_ref,
    count_ref,
    pair_ref,
    graph_ref,
    peram_ref,
    source_ref,
    sink_ref,
    load_sem,
    send_sem,
    recv_sem,
    edge_recv_sem,
):
    me = lax.axis_index("had")
    per_device, evecs, _ = source_ref.shape
    root_scale = 1.0 / math.sqrt(evecs)
    edge_scale = 1.0 / math.sqrt(evecs * graphs)
    sinks = sink_ref.shape[0]
    entries = graph_ref.shape[1]
    unroll = entries // ROUNDS

    def at(peer):
        return dict(device_id={"had": peer}, device_id_type=pl.DeviceIdType.MESH)

    barrier = pltpu.get_barrier_semaphore()
    for step in range(n - 1, 0, -1):
        pl.semaphore_signal(barrier, inc=1, **at(flip(me, step)))

    loads = {}
    for name, source, target in (
        ("pick", pick_in, pick_ref),
        ("peram", peram_in, peram_ref),
        ("source", source_in, source_ref),
        ("slot", slot_in, slot_ref),
        ("graph_sink", graph_sink_in, graph_sink_ref),
        ("count", count_in, count_ref),
        ("sink", sink_in, sink_ref),
        ("pair", pair_in, pair_ref),
    ):
        loads[name] = pltpu.make_async_copy(source, target, load_sem.at[len(loads)])
        loads[name].start()
    with jax.named_scope("load"):
        for name in ("pick", "peram", "source"):
            loads[name].wait()

    timeslice = me * per_device // evecs
    first = peram_ref[timeslice, 0]
    second = peram_ref[timeslice, 1]
    chips = n // 2
    levels = chips // 2
    chip, core = me // 2, me % 2
    level, row = chip // 2, chip % 2
    upper = chip // levels

    def across(distance, other_row):
        far = (1 - upper) * (chips // 2 - 1 - distance) + upper * distance
        return 2 * far + row + other_row * (1 - 2 * row)

    in_half = level % (levels // 2)
    inner = upper * (1 - in_half) + (1 - upper) * in_half

    def through(distance):
        return [
            (2 * across(distance, other) + side, levels + 2 * other + in_half)
            for side in range(2)
            for other in range(2)
        ]

    near = [flip(chip, step) for step in range(levels)]
    close = []
    for step in range(1, levels):
        close += [(2 * near[step] + 1 - core, step), (2 * near[step] + core, step)]
    first_order = through(0) + through(1)[:2] + close + through(1)[2:]
    second_order = close + through(0) + through(1)
    peers = [
        tuple(core * two + (1 - core) * one for one, two in zip(*both))
        for both in zip(first_order, second_order)
    ]
    peers += [(2 * chip + 1 - core, 0), (me, None)]

    def rotate(targets):
        halves = []
        for peer, _ in targets:
            slab = source_ref[pick_ref[0, peer]]
            half = jnp.dot(first, slab, preferred_element_type=jnp.float32)
            halves.append(half.astype(jnp.bfloat16))
        for (peer, _), half in zip(targets, halves):
            turned = lax.dot_general(half, second, NT, preferred_element_type=jnp.float32)
            target = received if peer is me else outgoing
            target[peer] = turned.astype(jnp.bfloat16)

    def send(targets):
        for peer, place in targets:
            if place is not None:
                pltpu.make_async_remote_copy(
                    src_ref=outgoing.at[peer],
                    dst_ref=received.at[me],
                    send_sem=send_sem.at[0],
                    recv_sem=recv_sem.at[place],
                    **at(peer),
                ).start()

    def arrival(buffer, semaphore):
        return pltpu.make_async_remote_copy(
            src_ref=buffer,
            dst_ref=buffer,
            send_sem=send_sem.at[0],
            recv_sem=semaphore,
            **at(2 * chip + 1 - core),
        )

    def all_sent(semaphore, slabs):
        pltpu.make_async_remote_copy(
            src_ref=table.at[pl.ds(0, slabs)],
            dst_ref=table.at[pl.ds(0, slabs)],
            send_sem=semaphore,
            recv_sem=recv_sem.at[0],
            **at(2 * chip + 1 - core),
        ).wait_send()

    group = 4
    for at_group in range(0, n, group):
        targets = peers[at_group : at_group + group]
        with jax.named_scope(f"rotate{at_group}"):
            rotate(targets)
        if at_group == 0:
            with jax.named_scope("meet"):
                pl.semaphore_wait(barrier, n - 1)
        send(targets)

    with jax.named_scope("index"):
        for name in ("slot", "graph_sink", "count"):
            loads[name].wait()
        graph_ids = lax.broadcasted_iota(jnp.int32, slot_ref.shape, 1)
        places = slot_ref[...] * sinks + graph_sink_ref[...]
        left_ids = jnp.where(graph_ids[:1] < count_ref[0], places[:1], n * sinks)
        for place, ids in enumerate(pair_up(left_ids, places[1:], n * sinks, entries)):
            index_ref[place : place + 1] = ids
        index_load = pltpu.make_async_copy(index_ref, graph_ref, load_sem.at[0])
        index_load.start()
        table[n * sinks] = jnp.zeros((evecs, evecs), jnp.bfloat16)
        rows = 4
        loads["sink"].wait()
        loads["pair"].wait()
        index_load.wait()


    def source(place, other):
        return 2 * ((1 - upper) * (levels // 2) + place) + row + other * (1 - 2 * row)

    from_near = [(near[step], step) for step in range(levels)]
    from_far = [
        (source(place, other), levels + 2 * other + place)
        for other in range(2)
        for place in (upper, 1 - upper)
    ]
    def fill(units, skip=0):
        places = [
            [inner * one + (1 - inner) * two for one, two in zip(*unit)] for unit in units
        ]
        for owner, semaphore in places[skip:]:
            landed = received.at[pl.ds(0, 2)]
            arrival(landed, recv_sem.at[semaphore]).wait_recv()
        for block in range(sinks // rows):
            left = sink_ref[block * rows : (block + 1) * rows].reshape(rows * evecs, evecs)
            for owner, _ in places:
                both = received[pl.ds(2 * owner, 2)].reshape(2 * evecs, evecs)
                product = lax.dot_general(left, both, NT, preferred_element_type=jnp.float32)
                factors = (product * root_scale).astype(jnp.bfloat16)
                for side in range(2):
                    part = factors[:, side * evecs : (side + 1) * evecs].reshape(rows, evecs, evecs)
                    table[pl.ds((2 * owner + side) * sinks + block * rows, rows)] = part

    with jax.named_scope("arrive0"):
        arrival(received.at[0], recv_sem.at[0]).wait_recv()
    order_inner = from_near + from_far
    order_outer = from_near[:2] + from_far + from_near[2:]
    units = list(zip(order_inner, order_outer))
    fill(units[:1], skip=1)
    with jax.named_scope("fill1"):
        fill(units[1:2])
    with jax.named_scope("fill2"):
        fill(units[2:3])
    with jax.named_scope("fill3"):
        fill(units[3:4])
    with jax.named_scope("fill4"):
        fill(units[4:6])
    with jax.named_scope("fill6"):
        fill(units[6:8])
    all_sent(send_sem.at[0], n - 1)

    def graph_step(block, total):
        start = unroll * block
        left = [table[graph_ref[0, start + entry]] for entry in range(unroll)]
        right = [
            jnp.concatenate([table[graph_ref[side, start + entry]] for side in (1, 2)], axis=1)
            for entry in range(unroll)
        ]
        both = jnp.dot(
            jnp.concatenate(left, axis=1),
            jnp.concatenate(right, axis=0),
            preferred_element_type=jnp.float32,
        )
        return total + both[:, :evecs] + both[:, evecs:]

    def edge_send(owners, count, peer, semaphore):
        pltpu.make_async_remote_copy(
            src_ref=edges.at[pl.ds(owners, count)],
            dst_ref=edges.at[pl.ds(owners, count)],
            send_sem=send_sem.at[0],
            recv_sem=edge_recv_sem.at[semaphore],
            **at(peer),
        ).start()

    my_place = 2 * (chip * (1 - upper) + (chips - 1 - chip) * upper) + upper

    def other_chip(turn):
        place = turn + (turn + chips - my_place) // chips
        return place % 2 * (chips - 1) + (1 - 2 * (place % 2)) * (place // 2)

    with jax.named_scope("graphs"):
        total = lax.fori_loop(0, ROUNDS, graph_step, jnp.zeros((evecs, evecs), jnp.float32))
        edge = (total * edge_scale).astype(jnp.bfloat16)
        edges[me] = edge
    landing = inner * (1 + core)
    far_outer = across(0, 0)
    ring = across(0, 1)

    @pl.when(inner == 1)
    def spread_inner():
        for turn in range(chips - 1):
            edge_send(me, 1, 2 * other_chip(turn) + 1, landing)

    @pl.when(inner == 0)
    def spread_outer():
        edge_send(me, 1, 2 * far_outer + 1, 0)
        edge_send(me, 1, 2 * ring + 1, 0)
        edge_send(me, 1, 2 * across(1, 0) + 1, 3)
        for target in near[1:]:
            edge_send(me, 1, 2 * target + 1, 0)

    @pl.when(core == 1)
    def to_first():
        edge_send(me, 1, me - 1, 0)

    @pl.when(core == 0)
    def to_second():
        edge_send(me, 1, me + 1, landing)

    edge_out[0] = edge

    inners = {1: [near[1], across(1, 0), across(1, 1)], 0: near[2:] + [across(1, 0), across(1, 1)]}
    outers = {1: near[2:] + [ring], 0: [near[1], far_outer, ring]}
    own = {1: (0, 1), 0: (1, 0)}
    relayed = {}

    def relay(kind):
        stages = [
            (3, 2, [(far_outer, 0, 2)]),
            (0, 2 * len(outers[kind]) + own[kind][0], [(chip_of, 0, 2) for chip_of in outers[kind]]),
            (1, len(inners[kind]) + own[kind][1], [(chip_of, 0, 1) for chip_of in inners[kind]]),
            (2, len(inners[kind]), [(chip_of, 1, 1) for chip_of in inners[kind]]),
        ]
        if kind == 0:
            stages = stages[1:]
        relayed[kind] = 2 * kind + sum(width for _, _, stage in stages for _, _, width in stage)
        for semaphore, count, stage in stages:
            with jax.named_scope(f"gather{semaphore}"):
                arrival(edges.at[pl.ds(0, count)], edge_recv_sem.at[semaphore]).wait_recv()
            for chip_of, side, width in stage:
                if semaphore == 3:
                    edge_send(2 * chip_of, width, 2 * near[1] + 1, 0)
                edge_send(2 * chip_of + side, width, me - 1, 0)

    for kind in range(2):
        pl.when((core == 1) & (inner == kind))(functools.partial(relay, kind))

    @pl.when(core == 0)
    def take_over():
        with jax.named_scope("partner0"):
            arrival(edges.at[pl.ds(0, n - 1)], edge_recv_sem.at[0]).wait_recv()

    with jax.named_scope("pairs"):
        for pair in range(product_out.shape[0]):
            product = jnp.dot(
                edges[pair_ref[0, pair]],
                edges[pair_ref[1, pair]],
                preferred_element_type=jnp.float32,
            )
            product_out[pair] = (product * root_scale).astype(jnp.bfloat16)

    for kind, spread in ((0, levels + 3), (1, chips)):
        for side in range(2):
            slabs = spread + side * relayed[kind]
            pl.when((core == side) & (inner == kind))(
                functools.partial(all_sent, send_sem.at[0], slabs)
            )


def store_kernel(edge_in, product_in, edge_out, product_out, store_sem):
    edge_copy = pltpu.make_async_copy(edge_in, edge_out, store_sem.at[0])
    product_copy = pltpu.make_async_copy(product_in, product_out, store_sem.at[1])
    edge_copy.start()
    product_copy.start()
    edge_copy.wait()
    product_copy.wait()


def fused_shards(
    n,
    source_slabs,
    sink_slabs,
    perambulators,
    send_pick,
    graph_slot,
    graph_sink,
    graph_count,
    pair_list,
):
    sinks, evecs, _ = sink_slabs.shape
    graphs = graph_slot.shape[1]
    pairs = pair_list.shape[0]
    entries = (graphs + n * sinks) // 2
    vmem = pl.BlockSpec(memory_space=pltpu.VMEM)
    hbm = pl.BlockSpec(memory_space=pltpu.HBM)
    slab = (evecs, evecs)
    held = pl.pallas_call(
        functools.partial(fused_kernel, n, graphs),
        out_shape=(
            pltpu.VMEM((1, *slab), jnp.bfloat16),
            pltpu.VMEM((pairs, *slab), jnp.bfloat16),
        ),
        in_specs=[hbm] * 8,
        out_specs=(vmem, vmem),
        scratch_shapes=[
            pltpu.VMEM((n, *slab), jnp.bfloat16),
            pltpu.VMEM((n, *slab), jnp.bfloat16),
            pltpu.VMEM((n, *slab), jnp.bfloat16),
            pltpu.VMEM((n * sinks + 1, *slab), jnp.bfloat16),
            pltpu.VMEM((2, graphs), jnp.int32),
            pltpu.VMEM((2, graphs), jnp.int32),
            pltpu.VMEM((4, entries), jnp.int32),
            pltpu.SMEM(send_pick.shape, jnp.int32),
            pltpu.SMEM((1,), jnp.int32),
            pltpu.SMEM((2, pairs), jnp.int32),
            pltpu.SMEM((4, entries), jnp.int32),
            pltpu.VMEM(perambulators.shape, jnp.bfloat16),
            pltpu.VMEM(source_slabs.shape, jnp.bfloat16),
            pltpu.VMEM(sink_slabs.shape, jnp.bfloat16),
            pltpu.SemaphoreType.DMA((8,)),
            pltpu.SemaphoreType.DMA((1,)),
            pltpu.SemaphoreType.DMA((n // 2,)),
            pltpu.SemaphoreType.DMA((4,)),
        ],
        compiler_params=pltpu.CompilerParams(
            collective_id=0, has_side_effects=True
        ),
        name="contraction",
    )(
        send_pick,
        graph_slot[0].T,
        graph_sink[0].T,
        graph_count,
        pair_list.T,
        perambulators,
        source_slabs,
        sink_slabs,
    )
    return pl.pallas_call(
        store_kernel,
        out_shape=tuple(jax.ShapeDtypeStruct(part.shape, part.dtype) for part in held),
        in_specs=[vmem, vmem],
        out_specs=(hbm, hbm),
        scratch_shapes=[pltpu.SemaphoreType.DMA((2,))],
        compiler_params=pltpu.CompilerParams(vmem_limit_bytes=1024 * 1024),
        name="store",
    )(*(pltpu.with_memory_space_constraint(part, pltpu.VMEM) for part in held))


def shards(readers, source_slabs, sink_slabs, perambulators, *tables):
    slabs = sink_slabs.shape[0]
    graphs = tables[1].shape[1]
    entries = (graphs + readers * slabs) // 2
    power = readers & (readers - 1) == 0 and readers // 8 == 2
    even = graphs % LANES == 0 and entries % (2 * ROUNDS) == 0 and entries % LANES == 0
    if power and even and readers * slabs <= 2 * graphs and slabs % 4 == 0:
        return fused_shards(readers, source_slabs, sink_slabs, perambulators, *tables)
    return looped_shards(source_slabs, sink_slabs, perambulators, *tables)


def solution(mesh):
    return jax.shard_map(
        functools.partial(shards, mesh.shape["had"]),
        mesh=mesh,
        in_specs=(
            P(("grp", "had"), None, None),
            P(("grp", "had"), None, None),
            P("grp", None, None, None),
            P(("grp", "had"), None),
            P(("grp", "had"), None, None),
            P(("grp", "had"), None, None),
            P(("grp", "had")),
            P(("grp", "had"), None),
        ),
        out_specs=(P(("grp", "had"), None, None), P(("grp", "had"), None, None)),
        check_vma=False,
    )
```
